32 devices in a mesh: space: 4 (over y, core), tm: 8 (over z, x).
Axes of the slice: x: 2, y: 2, z: 4, core: 2. Of those that a mesh axis runs over, the one named last changes fastest.
Arguments:
- snapshots: float32 [2048, 30720], P('tm', 'space'), may hold values from -6 to 6
- closing: float32 [128, 30720], P(None, 'space'), may hold values from -6 to 6
- weights: float32 [30720], P('space'), may hold values from 0.25 to 36, as said below
- bin_index: int32 [64], replicated, may hold values from 0 to 128, as said below
Outputs:
- spectra: float32 [64, 2, 16, 16], P('tm', None, 'space')
The draws below stay inside these ranges and needn't reach their ends.
Inputs may be any that keep to these rules, and one draw needn't show every extreme that they name: `bin_index`: distinct bins. Positive weights.
All inputs are finite; a program needn't handle non-finite values.
Results may differ from the reference program's by a relative error of at most 0.0003.
Values sent between devices are 32-bit elements; how exact they have to be, the bound alone decides.
A program may use at most 128 MiB of HBM per device.

```python
import jax
import jax.numpy as jnp
from jax import lax

NFFT = 256
NBINS = 64
P_DEV = 7680
EXTRA = 128
NBLK = 16
NT = 2048
NPTS = 30720
N_SPACE = 4


def draw_weights(key, part):
    position = jnp.arange(NPTS, dtype=jnp.float32) / (NPTS - 1)
    roughness = jnp.exp(jax.random.uniform(key, (NPTS,), jnp.float32, jnp.log(0.5), jnp.log(2.0)))
    return roughness * jnp.exp(jnp.log(3.0) * position)


def draw_bin_index(key, part):
    shuffled = jax.random.permutation(jax.random.fold_in(key, 11), NFFT // 2 + 1)
    return shuffled[:NBINS].astype(jnp.int32)


def level_of(key, dims, shards, smallest, high):
    factor_of = 1.0
    for dim, blocks in shards:
        heights = jax.random.uniform(jax.random.fold_in(jax.random.fold_in(key, 6), dim), (blocks,), jnp.float32, smallest / len(shards), high / len(shards))
        factor_of = factor_of * jnp.repeat(jnp.exp(heights), dims[dim] // blocks).reshape((-1,) + (1,) * (len(dims) - 1 - dim))
    return factor_of


def bell_draw(own_key, dims, deviation, reach, shards=(), kind=jnp.bfloat16):
    array = jax.random.normal(own_key, dims, jnp.float32) * deviation
    if len(shards) > 0:
        array = level_of(own_key, dims, shards, -0.22, 0.18) * array
    return jnp.clip(array, min=-reach, max=reach).astype(kind)


def setup_inputs(seed: int = 0) -> dict:
    key_list = jax.random.split(jax.random.key(seed), 5)
    snapshots = bell_draw(key_list[0], (NT, NPTS), 1.0, 6.0, ((0, 8), (1, 4)), jnp.float32)
    closing = bell_draw(key_list[1], (EXTRA, NPTS), 1.0, 6.0, ((1, 4),), jnp.float32)
    weights = draw_weights(jax.random.fold_in(key_list[4], 71), 0)
    bin_index = draw_bin_index(jax.random.fold_in(key_list[4], 71), 0)
    return {"snapshots": snapshots, "closing": closing, "weights": weights, "bin_index": bin_index}


def spectral_table(bin_index, length):
    sample = jnp.arange(length, dtype=jnp.int32)
    window = 0.5 - 0.5 * jnp.cos(2.0 * jnp.pi * sample.astype(jnp.float32) / length)
    phase_turns = (sample[:, None] * bin_index[None, :]) % length
    phase_angle = 2.0 * jnp.pi * phase_turns.astype(jnp.float32) / length
    paired = jnp.stack([window[:, None] * jnp.cos(phase_angle), -window[:, None] * jnp.sin(phase_angle)], axis=2)
    return paired.reshape(length, 2 * bin_index.shape[0])


def cross_spectra(first_set, second_set):
    products = jnp.einsum("kaip,kbjp->kabij", first_set, second_set, precision=lax.Precision.HIGHEST)
    real_part = products[:, 0, 0] + products[:, 1, 1]
    imag_part = products[:, 0, 1] - products[:, 1, 0]
    return jnp.stack([real_part, imag_part], axis=1)


def reference(snapshots, closing, weights, bin_index):
    basis_table = spectral_table(bin_index, NFFT)
    starts = jnp.arange(NBLK, dtype=jnp.int32) * (NFFT // 2)

    def group_sum(running, group_index):
        column_start = (group_index * P_DEV).astype(jnp.int32)
        columns = lax.dynamic_slice_in_dim(snapshots, column_start, P_DEV, 1)
        series = jnp.concatenate([columns, lax.dynamic_slice_in_dim(closing, column_start, P_DEV, 1)], axis=0)
        weight = lax.dynamic_slice_in_dim(weights, column_start, P_DEV, 0)

        def transform(begin_row):
            window_rows = lax.dynamic_slice_in_dim(series, begin_row, NFFT, 0)
            return lax.dot_general(basis_table, window_rows, (((0,), (0,)), ((), ())), precision=lax.Precision.HIGHEST)

        spectrum = lax.map(transform, starts)
        spectrum = spectrum.reshape(NBLK, NBINS, 2, P_DEV).transpose(1, 2, 0, 3)
        return running + cross_spectra(spectrum, spectrum * weight), None

    zeros_start = jnp.zeros((NBINS, 2, NBLK, NBLK), jnp.float32)
    cross_sum, unused = lax.scan(group_sum, zeros_start, jnp.arange(N_SPACE, dtype=jnp.int32))
    energy = jnp.trace(cross_sum[:, 0], axis1=1, axis2=2)
    return cross_sum * (NBLK / energy)[:, None, None, None]
```

```python
import functools

import jax
import jax.numpy as jnp
from jax import lax
from jax.experimental import pallas as pl
from jax.experimental.pallas import tpu as pltpu
from jax.sharding import PartitionSpec as P

NFFT = 256
NBINS = 64
LANES = 128
MESH = pl.DeviceIdType.MESH


def passed_along(array, axis, by):
    peers = lax.axis_size(axis)
    pairs = [(i, i + by) for i in range(peers) if 0 <= i + by < peers]
    return lax.ppermute(array, axis, pairs)


def spectral_table(bin_index, length):
    sample = jnp.arange(length, dtype=jnp.int32)
    window = 0.5 - 0.5 * jnp.cos(2.0 * jnp.pi * sample.astype(jnp.float32) / length)
    phase_turns = sample[:, None] * bin_index[None, :] % length
    phase_angle = 2.0 * jnp.pi * phase_turns.astype(jnp.float32) / length
    paired = jnp.stack(
        [window[:, None] * jnp.cos(phase_angle), -window[:, None] * jnp.sin(phase_angle)], axis=2
    )
    return paired.reshape(length, 2 * bin_index.shape[0])


def cross_spectra(first_set, second_set):
    products = jnp.einsum(
        "kaip,kbjp->kabij", first_set, second_set, precision=lax.Precision.HIGHEST
    )
    real_part = products[:, 0, 0] + products[:, 1, 1]
    imag_part = products[:, 0, 1] - products[:, 1, 0]
    return jnp.stack([real_part, imag_part], axis=1)


def body(snapshots, closing, weights, bin_index):
    stride_rows = NFFT // 2
    tail_rows = closing.shape[0]
    blocks_here = snapshots.shape[0] // stride_rows
    points = snapshots.shape[1]
    width_tm = lax.axis_size("tm")
    width_space = lax.axis_size("space")
    blocks_all = blocks_here * width_tm
    own_rows = blocks_all // width_space
    basis_table = spectral_table(bin_index, NFFT)
    incoming = passed_along(snapshots[:tail_rows], "tm", -1)
    last_device = lax.axis_index("tm") == width_tm - 1
    series = jnp.concatenate([snapshots, jnp.where(last_device, closing, incoming)], axis=0)
    leading = series[: blocks_here * stride_rows].reshape(blocks_here, stride_rows, points)
    trailing = series[stride_rows:].reshape(blocks_here, stride_rows, points)
    pieces = jnp.concatenate([leading, trailing], axis=1)
    spectrum = jnp.einsum("nc,bnp->cbp", basis_table, pieces, precision=lax.Precision.HIGHEST)
    spectrum = spectrum.reshape(NBINS, 2, blocks_here, points)
    gathered = lax.all_to_all(spectrum, "tm", split_axis=0, concat_axis=2, tiled=True)
    weighted = gathered * weights
    summed = lax.psum_scatter(
        cross_spectra(gathered, weighted).transpose(2, 0, 1, 3),
        "space",
        scatter_dimension=0,
        tiled=True,
    )
    row_ids = lax.axis_index("space") * own_rows + jnp.arange(own_rows, dtype=jnp.int32)
    diagonal = (row_ids[:, None] == jnp.arange(blocks_all, dtype=jnp.int32)[None, :]).astype(
        jnp.float32
    )
    local_trace = jnp.einsum(
        "rkj,rj->k", summed[:, :, 0, :], diagonal, precision=lax.Precision.HIGHEST
    )
    energy = lax.psum(local_trace, "space")
    spectra = summed * (blocks_all / energy)[None, :, None, None]
    return spectra.transpose(1, 2, 0, 3)


def tile_start(device, tiles, width_tm, space):
    return (device * tiles + (space % 2) * (width_tm // 2)) // width_tm


def halves(value):
    high = value.astype(jnp.bfloat16)
    return high, (value - high.astype(jnp.float32)).astype(jnp.bfloat16)


def matmul(a, b):
    return lax.dot_general(a, b, (((1,), (0,)), ((), ())), preferred_element_type=jnp.float32)


def matmul_nt(a, b):
    return lax.dot_general(a, b, (((1,), (1,)), ((), ())), preferred_element_type=jnp.float32)


def picked(selector, values):
    high, low = halves(values)
    return matmul(selector, high) + matmul(selector, low)


def picked_right(values, selector):
    high, low = halves(values)
    return matmul(high, selector) + matmul(low, selector)


def table_rows(bins, length):
    shape = (bins.shape[0], length)
    sample = lax.broadcasted_iota(jnp.int32, shape, 1)
    odd = (lax.broadcasted_iota(jnp.int32, shape, 0) & 1) == 1
    window = 0.5 - 0.5 * jnp.cos(2.0 * jnp.pi * sample.astype(jnp.float32) / length)
    turns = (sample * bins) & (length - 1)
    angle = 2.0 * jnp.pi * turns.astype(jnp.float32) / length
    return window * jnp.where(odd, -jnp.sin(angle), jnp.cos(angle))


def selections(blocks, group, width_space):
    own = blocks // width_space
    size = blocks * group
    line = lax.broadcasted_iota(jnp.int32, (4 * blocks, size), 0)
    lane = lax.broadcasted_iota(jnp.int32, (4 * blocks, size), 1)
    second = line >= 2 * blocks
    row = line & (2 * blocks - 1)
    imag = (row // own) & 1
    match = row // (2 * own) * own + (row & (own - 1)) == lane // group
    wanted = jnp.where(second, 1 - imag, imag)
    sign = jnp.where((imag == 1) & ~second, -1.0, 1.0)
    left = jnp.where(match & ((lane & 1) == wanted), sign, 0.0)
    line = lax.broadcasted_iota(jnp.int32, (size, blocks * group // 2), 0)
    lane = lax.broadcasted_iota(jnp.int32, (size, blocks * group // 2), 1)
    place = line // group * (group // 2) + (line & (group - 1)) // 2 == lane
    even = jnp.where(place & ((line & 1) == 0), 1.0, 0.0)
    odd = jnp.where(place & ((line & 1) == 1), 1.0, 0.0)
    return [m.astype(jnp.bfloat16) for m in (left, even, odd)]


def over_blocks(row, bins):
    shift = row.shape[1] // 2
    while shift >= bins:
        row = row + pltpu.roll(row, shift, 1)
        shift //= 2
    return row


def kernel(
    n,
    n_space,
    snap_ref,
    closing_ref,
    weights_ref,
    bins_ref,
    out_ref,
    series,
    table_ref,
    left_ref,
    even_ref,
    odd_ref,
    a_high,
    a_low,
    b_high,
    b_low,
    gram,
    part,
    rows_in,
    weights,
    bins,
    local_sem,
    send_sem,
    recv_sem,
    part_send,
    part_recv,
    round_sem,
):
    me = lax.axis_index("tm")
    here = lax.axis_index("space")
    rows, points = snap_ref.shape
    tail_rows = closing_ref.shape[0]
    tiles = points // LANES
    steps = series.shape[0]
    pairs = steps - 1
    hop = NFFT // 2
    blocks_all = n * rows // hop
    channels = 2 * bins_ref.shape[0]
    group = channels // n
    own_rows = blocks_all // n_space

    deep = n // 2
    z, x = me // 2, lax.rem(me, 2)
    near = me // deep * deep
    far = deep - near

    def peer_of(k):
        return lax.rem(me + k, n)

    def begin(device):
        return tile_start(device, tiles, n, here)

    my_start = begin(me)
    my_last = begin(me + 1) - my_start == 2 * steps

    def rows_of(device):
        return pl.ds(pl.multiple_of(device * rows, rows), rows)

    def columns(start, count):
        return pl.ds(pl.multiple_of(start * LANES, LANES), count * LANES)

    def pair_copy(step, peer, sender):
        return pltpu.make_async_remote_copy(
            src_ref=snap_ref.at[:, columns(begin(peer) + 2 * step, 2)],
            dst_ref=series.at[step, rows_of(sender)],
            send_sem=send_sem.at[step, peer],
            recv_sem=recv_sem.at[step, sender],
            device_id={"tm": peer},
            device_id_type=MESH,
        )

    def half_copy(half, peer, sender):
        return pltpu.make_async_remote_copy(
            src_ref=snap_ref.at[:, columns(begin(peer) + 2 * pairs + half, 1)],
            dst_ref=series.at[pairs, rows_of(sender), pl.ds(half * LANES, LANES)],
            send_sem=send_sem.at[pairs + half, peer],
            recv_sem=recv_sem.at[pairs + half, sender],
            device_id={"tm": peer},
            device_id_type=MESH,
        )

    def has_last(device):
        return begin(device + 1) - begin(device) == 2 * steps

    def own_pair(step):
        source = columns(my_start + 2 * step, 2)
        return (
            pltpu.make_async_copy(
                snap_ref.at[:, source], series.at[step, rows_of(me)], local_sem.at[0, step]
            ),
            pltpu.make_async_copy(
                closing_ref.at[:, source],
                series.at[step, pl.ds(n * rows, tail_rows)],
                local_sem.at[1, step],
            ),
        )

    def own_half(half):
        source = columns(my_start + 2 * pairs + half, 1)
        lanes = pl.ds(half * LANES, LANES)
        return (
            pltpu.make_async_copy(
                snap_ref.at[:, source],
                series.at[pairs, rows_of(me), lanes],
                local_sem.at[0, pairs + half],
            ),
            pltpu.make_async_copy(
                closing_ref.at[:, source],
                series.at[pairs, pl.ds(n * rows, tail_rows), lanes],
                local_sem.at[1, pairs + half],
            ),
        )

    weights_copy = pltpu.make_async_copy(weights_ref, weights, local_sem.at[2, 0])
    bins_copy = pltpu.make_async_copy(bins_ref, bins, local_sem.at[2, 1])

    def greet(sem):
        pl.semaphore_signal(sem, inc=1, device_id={"tm": me + 1 - 2 * x}, device_id_type=MESH)

        @pl.when(z + 1 < deep)
        def _():
            pl.semaphore_signal(sem, inc=1, device_id={"tm": me + 2}, device_id_type=MESH)

        @pl.when(z > 0)
        def _():
            pl.semaphore_signal(sem, inc=1, device_id={"tm": me - 2}, device_id_type=MESH)

        for other in (here + 1 - 2 * lax.rem(here, 2), lax.rem(here + 2, n_space)):
            pl.semaphore_signal(sem, inc=1, device_id={"space": other}, device_id_type=MESH)
        pl.semaphore_wait(sem, 3 + (z + 1 < deep).astype(jnp.int32) + (z > 0).astype(jnp.int32))

    def hops(peer):
        return jnp.abs(peer // 2 - z) + jnp.abs(lax.rem(peer, 2) - x)

    for reach in range(1, deep + 1):
        greet(pltpu.get_barrier_semaphore() if reach == 1 else round_sem.at[reach - 2])
        for k in range(1, n):
            peer = peer_of(k)

            @pl.when(hops(peer) == reach)
            def _(peer=peer):
                pair_copy(0, peer, me).start()

    @pl.loop(1, pairs)
    def _(step):
        for k in range(1, n):
            pair_copy(step, peer_of(k), me).start()

    for k in range(1, n):
        half_copy(0, peer_of(k), me).start()
    for k in range(1, n):

        @pl.when(has_last(peer_of(k)))
        def _(k=k):
            half_copy(1, peer_of(k), me).start()

    @pl.loop(0, pairs)
    def _(step):
        for copy in own_pair(step):
            copy.start()

    for copy in own_half(0):
        copy.start()

    @pl.when(my_last)
    def _():
        for copy in own_half(1):
            copy.start()

    weights_copy.start()
    bins_copy.start()
    for reach in range(deep + 1, deep + 3):
        greet(round_sem.at[reach - 2])

    gram[...] = jnp.zeros(gram.shape, jnp.float32)
    left_ref[...], even_ref[...], odd_ref[...] = selections(blocks_all, group, n_space)
    bins_copy.wait()
    channel = lax.broadcasted_iota(jnp.int32, (channels, 1), 0)
    held = jnp.zeros((channels, 1), jnp.int32)
    for k in range(channels // 2):
        held = jnp.where(channel // 2 == k, bins[k], held)
    table_high, table_low = halves(table_rows(held, NFFT))
    table_ref[:channels] = table_high
    table_ref[channels:] = table_low
    weights_copy.wait()

    def transform(step, lanes, weight):
        def run(turn, carry):
            block = lax.rem(near * (rows // hop) + turn, blocks_all)
            window = pl.ds(pl.multiple_of(block * hop, hop), NFFT)
            high, low = halves(series[step, window, lanes])
            both = matmul(table_ref[...], high)
            coef = both[:channels] + both[channels:] + matmul(table_ref[:channels], low)
            first_high, first_low = halves(coef)
            second_high, second_low = halves(coef * weight)
            place = pl.ds(pl.multiple_of(block * group, group), group)
            for g in range(n):
                cut = slice(g * group, (g + 1) * group)
                a_high[g, place, lanes] = first_high[cut]
                a_low[g, place, lanes] = first_low[cut]
                b_high[g, place, lanes] = second_high[cut]
                b_low[g, place, lanes] = second_low[cut]
            return carry

        return run

    def products(lanes):
        def run(g, carry):
            gram[g] += (
                matmul_nt(b_high[g, :, lanes], a_high[g, :, lanes])
                + matmul_nt(b_high[g, :, lanes], a_low[g, :, lanes])
                + matmul_nt(b_low[g, :, lanes], a_high[g, :, lanes])
            )
            return carry

        lax.fori_loop(0, n, run, 0, unroll=2)

    ready = blocks_all // 2 - 1

    def near_peer(k):
        return near + lax.rem(me - near + k, deep)

    @pl.loop(0, pairs)
    def _(step):
        weight = weights[pl.ds(pl.multiple_of((my_start + 2 * step) * LANES, LANES), 2 * LANES)]
        run = transform(step, slice(0, 2 * LANES), weight.reshape(1, 2 * LANES))
        for copy in own_pair(step):
            copy.wait()
        for k in range(1, deep):
            pair_copy(step, me, near_peer(k)).wait_recv()
        lax.fori_loop(0, ready, run, 0, unroll=ready)
        for k in range(deep):
            pair_copy(step, me, far + k).wait_recv()
        lax.fori_loop(ready, blocks_all, run, 0, unroll=3)
        products(slice(0, 2 * LANES))

    def last(half):
        lanes = slice(half * LANES, (half + 1) * LANES)
        tile = my_start + 2 * pairs + half
        weight = weights[pl.ds(pl.multiple_of(tile * LANES, LANES), LANES)]
        run = transform(pairs, lanes, weight.reshape(1, LANES))
        for copy in own_half(half):
            copy.wait()
        for k in range(1, deep):
            half_copy(half, me, near_peer(k)).wait_recv()
        lax.fori_loop(0, ready, run, 0, unroll=ready)
        for k in range(deep):
            half_copy(half, me, far + k).wait_recv()
            stop = blocks_all if k == deep - 1 else ready + 2 + 2 * k
            first = ready + 2 * k
            lax.fori_loop(first, stop, run, 0, unroll=stop - first)
        products(lanes)

    last(0)

    @pl.when(my_last)
    def _():
        last(1)

    size = gram.shape[1]
    row = lax.broadcasted_iota(jnp.int32, (size, size), 0)
    col = lax.broadcasted_iota(jnp.int32, (size, size), 1)
    same_bin = ((row & (group - 1)) >> 1) == ((col & (group - 1)) >> 1)
    line = lax.broadcasted_iota(jnp.int32, part.shape[1:], 0)
    lane = lax.broadcasted_iota(jnp.int32, part.shape[1:], 1)
    imag_row = ((line // own_rows) & 1) == 1
    on_diagonal = line // (2 * own_rows) * own_rows + (line & (own_rows - 1)) == lane // (group // 2)

    def folded(g):
        kept = picked(left_ref[...], jnp.where(same_bin, gram[g], 0.0))
        middle = kept.shape[0] // 2
        sums = picked_right(kept[:middle], even_ref[...]) + picked_right(
            kept[middle:], odd_ref[...]
        )
        real = jnp.where(on_diagonal & ~imag_row, sums, 0.0)
        trace = over_blocks(jnp.sum(real, axis=0, keepdims=True), group // 2)
        part[g] = jnp.where(on_diagonal & imag_row, trace, sums)

    own_lines = 2 * own_rows

    def part_copy(peer, there, sender, sender_space):
        return pltpu.make_async_remote_copy(
            src_ref=part.at[peer, pl.ds(pl.multiple_of(there * own_lines, own_lines), own_lines)],
            dst_ref=rows_in.at[sender, sender_space],
            send_sem=part_send.at[peer, there],
            recv_sem=part_recv.at[sender, sender_space],
            device_id={"tm": peer, "space": there},
            device_id_type=MESH,
        )

    def others(k):
        return [lax.rem(here + j, n_space) for j in range(1 if k == 0 else 0, n_space)]

    order = [far + k for k in range(deep)] + [near_peer(k) for k in range(1, deep)]
    for peer in order:
        folded(peer)
        for there in others(1):
            part_copy(peer, there, me, here).start()
    folded(me)
    for there in others(0):
        part_copy(me, there, me, here).start()
    rows_in[me, here] = part[me, pl.ds(pl.multiple_of(here * own_lines, own_lines), own_lines)]
    for there in others(0):
        part_copy(me, here, me, there).wait_recv()
    for peer in order:
        for there in others(1):
            part_copy(me, here, peer, there).wait_recv()
    total = rows_in[0, 0]
    for p in range(n):
        for q in range(n_space):
            if p + q > 0:
                total = total + rows_in[p, q]
    line = lax.broadcasted_iota(jnp.int32, total.shape, 0)
    block = lax.broadcasted_iota(jnp.int32, total.shape, 1) // (group // 2)
    first = (line == own_rows) & (block == here * own_rows)
    held = jnp.sum(jnp.where(first, total, 0.0), axis=0, keepdims=True)
    energy = over_blocks(held, group // 2)
    zero = (line >= own_rows) & (block == here * own_rows + (line & (own_rows - 1)))
    out_ref[...] = jnp.where(zero, 0.0, total) * (blocks_all / energy)

    @pl.loop(0, pairs)
    def _(step):
        for k in range(1, n):
            pair_copy(step, peer_of(k), me).wait_send()

    for k in range(1, n):
        half_copy(0, peer_of(k), me).wait_send()

        @pl.when(has_last(peer_of(k)))
        def _(k=k):
            half_copy(1, peer_of(k), me).wait_send()

    for peer in order:
        for there in others(1):
            part_copy(peer, there, me, here).wait_send()
    for there in others(0):
        part_copy(me, there, me, here).wait_send()


def fused_body(snapshots, closing, weights, bin_index):
    n, n_space = lax.axis_size("tm"), lax.axis_size("space")
    rows, points = snapshots.shape
    tail_rows = closing.shape[0]
    tiles = points // LANES
    steps = -(-tiles // n) // 2
    blocks_all = n * rows // (NFFT // 2)
    channels = 2 * bin_index.shape[0]
    group = channels // n
    size = blocks_all * group
    own_rows = blocks_all // n_space
    shape = (2 * own_rows, size // 2)
    sums = pl.pallas_call(
        functools.partial(kernel, n, n_space),
        out_shape=jax.ShapeDtypeStruct(shape, jnp.float32),
        in_specs=[pl.BlockSpec(memory_space=pl.ANY)] * 4,
        out_specs=pl.BlockSpec(memory_space=pltpu.VMEM),
        scratch_shapes=[
            pltpu.VMEM((steps, n * rows + tail_rows, 2 * LANES), jnp.float32),
            pltpu.VMEM((2 * channels, NFFT), jnp.bfloat16),
            pltpu.VMEM((4 * blocks_all, size), jnp.bfloat16),
            pltpu.VMEM((size, size // 2), jnp.bfloat16),
            pltpu.VMEM((size, size // 2), jnp.bfloat16),
        ]
        + [pltpu.VMEM((n, size, 2 * LANES), jnp.bfloat16)] * 4
        + [
            pltpu.VMEM((n, size, size), jnp.float32),
            pltpu.VMEM((n, 2 * blocks_all, size // 2), jnp.float32),
            pltpu.VMEM((n, n_space) + shape, jnp.float32),
            pltpu.VMEM((points,), jnp.float32),
            pltpu.SMEM((channels // 2,), jnp.int32),
            pltpu.SemaphoreType.DMA((3, steps + 1)),
            pltpu.SemaphoreType.DMA((steps + 1, n)),
            pltpu.SemaphoreType.DMA((steps + 1, n)),
            pltpu.SemaphoreType.DMA((n, n_space)),
            pltpu.SemaphoreType.DMA((n, n_space)),
            pltpu.SemaphoreType.REGULAR((n // 2 + 1,)),
        ],
        compiler_params=pltpu.CompilerParams(collective_id=0, has_side_effects=True),
    )(snapshots, closing, weights, bin_index)
    by_pair = sums.reshape(2, own_rows, blocks_all, group // 2)
    return by_pair.transpose(3, 0, 1, 2)


def chosen_body(snapshots, closing, weights, bin_index):
    n, n_space = lax.axis_size("tm"), lax.axis_size("space")
    rows, points = snapshots.shape
    group = 2 * NBINS // n
    blocks_all = n * rows // (NFFT // 2)
    tiles = points // LANES
    slots = -(-tiles // n)
    fits = (
        2 * NBINS % n == 0
        and n % 2 == 0
        and n_space == 4
        and points % LANES == 0
        and slots % 2 == 0
        and slots > 2
        and tiles // n >= slots - 1
        and closing.shape[0] == NFFT // 2
        and rows == NFFT
        and group == 16
        and blocks_all == 16
    )
    return (fused_body if fits else body)(snapshots, closing, weights, bin_index)


def solution(mesh):
    return jax.shard_map(
        chosen_body,
        mesh=mesh,
        in_specs=(P("tm", "space"), P(None, "space"), P("space"), P()),
        out_specs=P("tm", None, "space", None),
        check_vma=False,
    )
```

```python
import functools

import jax
import jax.numpy as jnp
from jax import lax
from jax.experimental import pallas as pl
from jax.experimental.pallas import tpu as pltpu
from jax.sharding import PartitionSpec as P

NFFT = 256
NBINS = 64
LANES = 128
MESH = pl.DeviceIdType.MESH


def passed_along(array, axis, by):
    peers = lax.axis_size(axis)
    pairs = [(i, i + by) for i in range(peers) if 0 <= i + by < peers]
    return lax.ppermute(array, axis, pairs)


def spectral_table(bin_index, length):
    sample = jnp.arange(length, dtype=jnp.int32)
    window = 0.5 - 0.5 * jnp.cos(2.0 * jnp.pi * sample.astype(jnp.float32) / length)
    phase_turns = sample[:, None] * bin_index[None, :] % length
    phase_angle = 2.0 * jnp.pi * phase_turns.astype(jnp.float32) / length
    paired = jnp.stack(
        [window[:, None] * jnp.cos(phase_angle), -window[:, None] * jnp.sin(phase_angle)], axis=2
    )
    return paired.reshape(length, 2 * bin_index.shape[0])


def cross_spectra(first_set, second_set):
    products = jnp.einsum(
        "kaip,kbjp->kabij", first_set, second_set, precision=lax.Precision.HIGHEST
    )
    real_part = products[:, 0, 0] + products[:, 1, 1]
    imag_part = products[:, 0, 1] - products[:, 1, 0]
    return jnp.stack([real_part, imag_part], axis=1)


def body(snapshots, closing, weights, bin_index):
    stride_rows = NFFT // 2
    tail_rows = closing.shape[0]
    blocks_here = snapshots.shape[0] // stride_rows
    points = snapshots.shape[1]
    width_tm = lax.axis_size("tm")
    width_space = lax.axis_size("space")
    blocks_all = blocks_here * width_tm
    own_rows = blocks_all // width_space
    basis_table = spectral_table(bin_index, NFFT)
    incoming = passed_along(snapshots[:tail_rows], "tm", -1)
    last_device = lax.axis_index("tm") == width_tm - 1
    series = jnp.concatenate([snapshots, jnp.where(last_device, closing, incoming)], axis=0)
    leading = series[: blocks_here * stride_rows].reshape(blocks_here, stride_rows, points)
    trailing = series[stride_rows:].reshape(blocks_here, stride_rows, points)
    pieces = jnp.concatenate([leading, trailing], axis=1)
    spectrum = jnp.einsum("nc,bnp->cbp", basis_table, pieces, precision=lax.Precision.HIGHEST)
    spectrum = spectrum.reshape(NBINS, 2, blocks_here, points)
    gathered = lax.all_to_all(spectrum, "tm", split_axis=0, concat_axis=2, tiled=True)
    weighted = gathered * weights
    summed = lax.psum_scatter(
        cross_spectra(gathered, weighted).transpose(2, 0, 1, 3),
        "space",
        scatter_dimension=0,
        tiled=True,
    )
    row_ids = lax.axis_index("space") * own_rows + jnp.arange(own_rows, dtype=jnp.int32)
    diagonal = (row_ids[:, None] == jnp.arange(blocks_all, dtype=jnp.int32)[None, :]).astype(
        jnp.float32
    )
    local_trace = jnp.einsum(
        "rkj,rj->k", summed[:, :, 0, :], diagonal, precision=lax.Precision.HIGHEST
    )
    energy = lax.psum(local_trace, "space")
    spectra = summed * (blocks_all / energy)[None, :, None, None]
    return spectra.transpose(1, 2, 0, 3)


def halves(value):
    high = value.astype(jnp.bfloat16)
    return high, (value - high.astype(jnp.float32)).astype(jnp.bfloat16)


def matmul(a, b):
    return lax.dot_general(a, b, (((1,), (0,)), ((), ())), preferred_element_type=jnp.float32)


def matmul_nt(a, b):
    return lax.dot_general(a, b, (((1,), (1,)), ((), ())), preferred_element_type=jnp.float32)


def picked(selector, values):
    high, low = halves(values)
    return matmul(selector, high) + matmul(selector, low)


def picked_right(values, selector):
    high, low = halves(values)
    return matmul(high, selector) + matmul(low, selector)


def table_rows(bins, length):
    shape = (bins.shape[0], length)
    sample = lax.broadcasted_iota(jnp.int32, shape, 1)
    odd = (lax.broadcasted_iota(jnp.int32, shape, 0) & 1) == 1
    window = 0.5 - 0.5 * jnp.cos(2.0 * jnp.pi * sample.astype(jnp.float32) / length)
    turns = (sample * bins) & (length - 1)
    angle = 2.0 * jnp.pi * turns.astype(jnp.float32) / length
    return window * jnp.where(odd, -jnp.sin(angle), jnp.cos(angle))


def selections(blocks, group, width_space):
    own = blocks // width_space
    size = blocks * group
    line = lax.broadcasted_iota(jnp.int32, (4 * blocks, size), 0)
    lane = lax.broadcasted_iota(jnp.int32, (4 * blocks, size), 1)
    second = line >= 2 * blocks
    row = line & (2 * blocks - 1)
    imag = (row // own) & 1
    match = row // (2 * own) * own + (row & (own - 1)) == lane // group
    wanted = jnp.where(second, 1 - imag, imag)
    sign = jnp.where((imag == 1) & ~second, -1.0, 1.0)
    left = jnp.where(match & ((lane & 1) == wanted), sign, 0.0)
    line = lax.broadcasted_iota(jnp.int32, (size, blocks * group // 2), 0)
    lane = lax.broadcasted_iota(jnp.int32, (size, blocks * group // 2), 1)
    place = line // group * (group // 2) + (line & (group - 1)) // 2 == lane
    even = jnp.where(place & ((line & 1) == 0), 1.0, 0.0)
    odd = jnp.where(place & ((line & 1) == 1), 1.0, 0.0)
    return [m.astype(jnp.bfloat16) for m in (left, even, odd)]


def over_blocks(row, bins):
    shift = row.shape[1] // 2
    while shift >= bins:
        row = row + pltpu.roll(row, shift, 1)
        shift //= 2
    return row


def kernel(
    n,
    n_space,
    snap_ref,
    closing_ref,
    weights_ref,
    bins_ref,
    out_ref,
    series,
    late_series,
    table_ref,
    left_ref,
    even_ref,
    odd_ref,
    a_high,
    a_low,
    b_high,
    b_low,
    late_a_high,
    late_a_low,
    late_b_high,
    late_b_low,
    gram,
    coef_out,
    coef_in,
    edge_out,
    edge_in,
    part,
    space_in,
    rows_out,
    rows_in,
    late_part,
    late_in,
    weights,
    bins,
    local_sem,
    send_sem,
    recv_sem,
    halo_sem,
    space_send,
    space_recv,
    rows_send,
    rows_recv,
    late_send,
    late_recv,
    round_sem,
):
    me = lax.axis_index("tm")
    here = lax.axis_index("space")
    rows, points = snap_ref.shape
    tail_rows = closing_ref.shape[0]
    tiles = points // LANES
    each = tiles // n
    pairs = each // 2
    late_tiles = tiles - each * n
    hop = NFFT // 2
    blocks_here = rows // hop
    blocks_all = n * blocks_here
    channels = 2 * bins_ref.shape[0]
    group = channels // n
    own_rows = blocks_all // n_space
    own_lines = 2 * own_rows
    held_rows = blocks_here * group

    deep = n // 2
    z, x = me // 2, lax.rem(me, 2)
    near = me // deep * deep
    far = deep - near
    near_peers = [near + lax.rem(me - near + k, deep) for k in range(1, deep)]
    far_peers = [far + lax.rem(me - near + k, deep) for k in range(deep)]
    peers = far_peers + near_peers
    space_peers = [lax.rem(here + k, n_space) for k in range(1, n_space)]

    def rows_of(device):
        return pl.ds(pl.multiple_of(device * rows, rows), rows)

    def columns(start, count):
        return pl.ds(pl.multiple_of(start * LANES, LANES), count * LANES)

    late_columns = pl.ds(each * n * LANES, late_tiles * LANES)

    def to_tm(src, dst, kind, peer, sender):
        return pltpu.make_async_remote_copy(
            src_ref=src,
            dst_ref=dst,
            send_sem=send_sem.at[kind, peer],
            recv_sem=recv_sem.at[kind, sender],
            device_id={"tm": peer},
            device_id_type=MESH,
        )

    def pair_copy(step, peer, sender):
        source = columns(peer * each + 2 * step, 2)
        return to_tm(
            snap_ref.at[:, source], series.at[step, rows_of(sender)], step, peer, sender
        )

    def single_copy(peer, sender):
        source = columns(peer * each + 2 * pairs, 1)
        target = series.at[pairs, rows_of(sender), pl.ds(0, LANES)]
        return to_tm(snap_ref.at[:, source], target, pairs, peer, sender)

    def coef_copy(peer, sender):
        target = coef_in.at[pl.ds(pl.multiple_of(sender * held_rows, held_rows), held_rows)]
        return to_tm(coef_out.at[peer], target, pairs + 1, peer, sender)

    def edge_copy(peer):
        return to_tm(edge_out.at[peer], edge_in, pairs + 2, peer, deep)

    halo_copy = pltpu.make_async_remote_copy(
        src_ref=snap_ref.at[pl.ds(0, tail_rows), late_columns],
        dst_ref=late_series.at[pl.ds(rows, tail_rows)],
        send_sem=halo_sem.at[0],
        recv_sem=halo_sem.at[1],
        device_id={"tm": lax.rem(me + n - 1, n)},
        device_id_type=MESH,
    )
    gives_halo = (me != 0) & (me != deep)
    takes_halo = (me != n - 1) & (me != deep - 1)

    def own_copies(step):
        single = isinstance(step, int) and step == pairs
        source = columns(me * each + 2 * step, 1 if single else 2)
        lanes = pl.ds(0, LANES if single else 2 * LANES)
        return (
            pltpu.make_async_copy(
                snap_ref.at[:, source], series.at[step, rows_of(me), lanes], local_sem.at[0, step]
            ),
            pltpu.make_async_copy(
                closing_ref.at[:, source],
                series.at[step, pl.ds(n * rows, tail_rows), lanes],
                local_sem.at[1, step],
            ),
        )

    late_own = pltpu.make_async_copy(
        snap_ref.at[:, late_columns], late_series.at[pl.ds(0, rows)], local_sem.at[2, 0]
    )
    late_closing = pltpu.make_async_copy(
        closing_ref.at[:, late_columns],
        late_series.at[pl.ds(rows, tail_rows)],
        local_sem.at[2, 1],
    )
    weights_copy = pltpu.make_async_copy(weights_ref, weights, local_sem.at[2, 2])
    bins_copy = pltpu.make_async_copy(bins_ref, bins, local_sem.at[2, 3])

    def greet(sem):
        pl.semaphore_signal(sem, inc=1, device_id={"tm": me + 1 - 2 * x}, device_id_type=MESH)

        @pl.when(z + 1 < deep)
        def _():
            pl.semaphore_signal(sem, inc=1, device_id={"tm": me + 2}, device_id_type=MESH)

        @pl.when(z > 0)
        def _():
            pl.semaphore_signal(sem, inc=1, device_id={"tm": me - 2}, device_id_type=MESH)

        for other in (here + 1 - 2 * lax.rem(here, 2), lax.rem(here + 2, n_space)):
            pl.semaphore_signal(sem, inc=1, device_id={"space": other}, device_id_type=MESH)
        pl.semaphore_wait(sem, 3 + (z + 1 < deep).astype(jnp.int32) + (z > 0).astype(jnp.int32))

    def hops(peer):
        return jnp.abs(peer // 2 - z) + jnp.abs(lax.rem(peer, 2) - x)

    for reach in range(1, deep + 1):
        greet(pltpu.get_barrier_semaphore() if reach == 1 else round_sem.at[reach - 2])
        for peer in peers:

            @pl.when(hops(peer) == reach)
            def _(peer=peer):
                pair_copy(0, peer, me).start()

        if reach == 2:

            @pl.when(gives_halo)
            def _():
                halo_copy.start()

    for step in range(1, pairs):
        for peer in near_peers + far_peers:
            pair_copy(step, peer, me).start()
    for peer in near_peers:
        single_copy(peer, me).start()

    bins_copy.start()
    late_own.start()

    @pl.when(me == n - 1)
    def _():
        late_closing.start()

    weights_copy.start()

    for step in range(pairs + 1):
        for copy in own_copies(step):
            copy.start()

    @pl.when(me == deep - 1)
    def _():
        late_series[rows:] = jnp.zeros((tail_rows, late_series.shape[1]), jnp.float32)

    gram[...] = jnp.zeros(gram.shape, jnp.float32)
    left_ref[...], even_ref[...], odd_ref[...] = selections(blocks_all, group, n_space)
    bins_copy.wait()
    channel = lax.broadcasted_iota(jnp.int32, (channels, 1), 0)
    held = jnp.zeros((channels, 1), jnp.int32)
    for k in range(channels // 2):
        held = jnp.where(channel // 2 == k, bins[k], held)
    table_high, table_low = halves(table_rows(held, NFFT))
    table_ref[:channels] = table_high
    table_ref[channels:] = table_low
    weights_copy.wait()

    def transformed(piece):
        high, low = halves(piece)
        both = matmul(table_ref[...], high)
        return both[:channels] + both[channels:] + matmul(table_ref[:channels], low)

    late_own.wait()

    @pl.when(takes_halo)
    def _():
        halo_copy.wait_recv()

    @pl.when(me == n - 1)
    def _():
        late_closing.wait()

    for block in range(blocks_here):
        coef = transformed(late_series[block * hop : block * hop + NFFT])
        for g in range(n):
            coef_out[g, block * group : (block + 1) * group] = coef[g * group : (g + 1) * group]
    coef_in[pl.ds(pl.multiple_of(me * held_rows, held_rows), held_rows)] = coef_out[me]

    @pl.when(me == deep)
    def _():
        begun = late_series[:hop]
        coef = transformed(jnp.concatenate([jnp.zeros_like(begun), begun], axis=0))
        for g in range(n):
            edge_out[g] = coef[g * group : (g + 1) * group]
        edge_in[...] = edge_out[me]

    def transform(step, lanes, weight):
        def run(turn, carry):
            block = lax.rem(near * blocks_here + turn, blocks_all)
            window = pl.ds(pl.multiple_of(block * hop, hop), NFFT)
            coef = transformed(series[step, window, lanes])
            first_high, first_low = halves(coef)
            second_high, second_low = halves(coef * weight)
            place = pl.ds(pl.multiple_of(block * group, group), group)
            for g in range(n):
                cut = slice(g * group, (g + 1) * group)
                a_high[g, place, lanes] = first_high[cut]
                a_low[g, place, lanes] = first_low[cut]
                b_high[g, place, lanes] = second_high[cut]
                b_low[g, place, lanes] = second_low[cut]
            return carry

        return run

    def products(lanes):
        def run(g, carry):
            gram[g] += (
                matmul_nt(b_high[g, :, lanes], a_high[g, :, lanes])
                + matmul_nt(b_high[g, :, lanes], a_low[g, :, lanes])
                + matmul_nt(b_low[g, :, lanes], a_high[g, :, lanes])
            )
            return carry

        lax.fori_loop(0, n, run, 0, unroll=2)

    ready = blocks_all // 2 - 1

    @pl.loop(0, pairs)
    def _(step):
        @pl.when(step == 1)
        def _():
            for peer in near_peers:
                coef_copy(peer, me).start()

            @pl.when(me == deep)
            def _():
                for peer in near_peers:
                    edge_copy(peer).start()

            for peer in far_peers:
                single_copy(peer, me).start()
            for peer in far_peers:
                coef_copy(peer, me).start()

            @pl.when(me == deep)
            def _():
                for peer in far_peers:
                    edge_copy(peer).start()

        start = pl.multiple_of((me * each + 2 * step) * LANES, LANES)
        weight = weights[pl.ds(start, 2 * LANES)].reshape(1, 2 * LANES)
        run = transform(step, slice(0, 2 * LANES), weight)
        for copy in own_copies(step):
            copy.wait()
        for peer in near_peers:
            pair_copy(step, me, peer).wait_recv()
        lax.fori_loop(0, ready, run, 0, unroll=ready)
        for k in range(deep):
            pair_copy(step, me, far + k).wait_recv()
        lax.fori_loop(ready, blocks_all, run, 0, unroll=3)
        products(slice(0, 2 * LANES))

    start = pl.multiple_of((me * each + 2 * pairs) * LANES, LANES)
    run = transform(pairs, slice(0, LANES), weights[pl.ds(start, LANES)].reshape(1, LANES))
    for copy in own_copies(pairs):
        copy.wait()
    for peer in near_peers:
        single_copy(me, peer).wait_recv()
    lax.fori_loop(0, ready, run, 0, unroll=ready)
    for k in range(deep):
        single_copy(me, far + k).wait_recv()
        stop = blocks_all if k == deep - 1 else ready + 2 + 2 * k
        first = ready + 2 * k
        lax.fori_loop(first, stop, run, 0, unroll=stop - first)
    products(slice(0, LANES))

    size = gram.shape[1]
    row = lax.broadcasted_iota(jnp.int32, (size, size), 0)
    col = lax.broadcasted_iota(jnp.int32, (size, size), 1)
    same_bin = ((row & (group - 1)) >> 1) == ((col & (group - 1)) >> 1)
    line = lax.broadcasted_iota(jnp.int32, late_part.shape, 0)
    lane = lax.broadcasted_iota(jnp.int32, late_part.shape, 1)
    imag_row = ((line // own_rows) & 1) == 1
    on_diagonal = line // own_lines * own_rows + (line & (own_rows - 1)) == lane // (group // 2)

    def folded(values):
        kept = picked(left_ref[...], jnp.where(same_bin, values, 0.0))
        middle = kept.shape[0] // 2
        sums = picked_right(kept[:middle], even_ref[...]) + picked_right(
            kept[middle:], odd_ref[...]
        )
        real = jnp.where(on_diagonal & ~imag_row, sums, 0.0)
        trace = over_blocks(jnp.sum(real, axis=0, keepdims=True), group // 2)
        return jnp.where(on_diagonal & imag_row, trace, sums)

    def fold(g, carry):
        sums = folded(gram[g])
        for s in range(n_space):
            part[s, g] = sums[s * own_lines : (s + 1) * own_lines]
        return carry

    lax.fori_loop(0, n, fold, 0, unroll=2)

    def space_copy(peer, sender):
        return pltpu.make_async_remote_copy(
            src_ref=part.at[peer],
            dst_ref=space_in.at[sender],
            send_sem=space_send.at[peer],
            recv_sem=space_recv.at[sender],
            device_id={"space": peer},
            device_id_type=MESH,
        )

    def rows_copy(peer, sender):
        return pltpu.make_async_remote_copy(
            src_ref=rows_out.at[peer],
            dst_ref=rows_in.at[sender],
            send_sem=rows_send.at[peer],
            recv_sem=rows_recv.at[sender],
            device_id={"tm": peer},
            device_id_type=MESH,
        )

    def late_copy(peer, sender):
        source = pl.ds(pl.multiple_of(peer * own_lines, own_lines), own_lines)
        return pltpu.make_async_remote_copy(
            src_ref=late_part.at[source],
            dst_ref=late_in.at[sender],
            send_sem=late_send.at[peer],
            recv_sem=late_recv.at[sender],
            device_id={"space": peer},
            device_id_type=MESH,
        )

    for peer in space_peers:
        space_copy(peer, here).start()
    space_in[here] = part[here]
    for peer in space_peers:
        space_copy(here, peer).wait_recv()
    total = space_in[0]
    for s in range(1, n_space):
        total = total + space_in[s]
    rows_out[...] = total
    rows_in[me] = rows_out[me]
    for peer in peers:
        rows_copy(peer, me).start()

    late_weight = weights[pl.ds(each * n * LANES, late_tiles * LANES)]
    late_weight = late_weight.reshape(1, late_tiles * LANES)

    def take(sender, straddles=False):
        @pl.when(sender != me)
        def _():
            coef_copy(me, sender).wait_recv()

        place = pl.ds(pl.multiple_of(sender * held_rows, held_rows), held_rows)
        coef = coef_in[place]
        if straddles:

            @pl.when(me != deep)
            def _():
                edge_copy(me).wait_recv()

            coef = jnp.concatenate(
                [coef[: held_rows - group], coef[held_rows - group :] + edge_in[...]], axis=0
            )
        late_a_high[place], late_a_low[place] = halves(coef)
        late_b_high[place], late_b_low[place] = halves(coef * late_weight)

    for k in range(deep - 1):
        take(near + k)
    for k in range(deep - 1):
        take(far + k)
    take(jnp.int32(n - 1))
    take(jnp.int32(deep - 1), straddles=True)
    late_part[...] = folded(
        matmul_nt(late_b_high[...], late_a_high[...])
        + matmul_nt(late_b_high[...], late_a_low[...])
        + matmul_nt(late_b_low[...], late_a_high[...])
    )
    for peer in space_peers:
        late_copy(peer, here).start()
    late_in[here] = late_part[pl.ds(pl.multiple_of(here * own_lines, own_lines), own_lines)]
    for peer in peers:
        rows_copy(me, peer).wait_recv()
    total = rows_in[0]
    for p in range(1, n):
        total = total + rows_in[p]
    for peer in space_peers:
        late_copy(here, peer).wait_recv()
    for s in range(n_space):
        total = total + late_in[s]
    line = lax.broadcasted_iota(jnp.int32, total.shape, 0)
    block = lax.broadcasted_iota(jnp.int32, total.shape, 1) // (group // 2)
    first = (line == own_rows) & (block == here * own_rows)
    held = jnp.sum(jnp.where(first, total, 0.0), axis=0, keepdims=True)
    energy = over_blocks(held, group // 2)
    zero = (line >= own_rows) & (block == here * own_rows + (line & (own_rows - 1)))
    out_ref[...] = jnp.where(zero, 0.0, total) * (blocks_all / energy)

    for peer in peers:
        for step in range(pairs):
            pair_copy(step, peer, me).wait_send()
        single_copy(peer, me).wait_send()
        coef_copy(peer, me).wait_send()
        rows_copy(peer, me).wait_send()

    @pl.when(gives_halo)
    def _():
        halo_copy.wait_send()

    @pl.when(me == deep)
    def _():
        for peer in peers:
            edge_copy(peer).wait_send()

    for peer in space_peers:
        space_copy(peer, here).wait_send()
        late_copy(peer, here).wait_send()


def fused_body(snapshots, closing, weights, bin_index):
    n, n_space = lax.axis_size("tm"), lax.axis_size("space")
    rows, points = snapshots.shape
    tail_rows = closing.shape[0]
    tiles = points // LANES
    each = tiles // n
    pairs = each // 2
    late = (tiles - each * n) * LANES
    blocks_all = n * rows // (NFFT // 2)
    channels = 2 * bin_index.shape[0]
    group = channels // n
    size = blocks_all * group
    own_lines = 2 * blocks_all // n_space
    shape = (own_lines, size // 2)
    sums = pl.pallas_call(
        functools.partial(kernel, n, n_space),
        out_shape=jax.ShapeDtypeStruct(shape, jnp.float32),
        in_specs=[pl.BlockSpec(memory_space=pl.ANY)] * 4,
        out_specs=pl.BlockSpec(memory_space=pltpu.VMEM),
        scratch_shapes=[
            pltpu.VMEM((pairs + 1, n * rows + tail_rows, 2 * LANES), jnp.float32),
            pltpu.VMEM((rows + tail_rows, late), jnp.float32),
            pltpu.VMEM((2 * channels, NFFT), jnp.bfloat16),
            pltpu.VMEM((4 * blocks_all, size), jnp.bfloat16),
            pltpu.VMEM((size, size // 2), jnp.bfloat16),
            pltpu.VMEM((size, size // 2), jnp.bfloat16),
        ]
        + [pltpu.VMEM((n, size, 2 * LANES), jnp.bfloat16)] * 4
        + [pltpu.VMEM((size, late), jnp.bfloat16)] * 4
        + [
            pltpu.VMEM((n, size, size), jnp.float32),
            pltpu.VMEM((n, size // n, late), jnp.float32),
            pltpu.VMEM((size, late), jnp.float32),
            pltpu.VMEM((n, group, late), jnp.float32),
            pltpu.VMEM((group, late), jnp.float32),
            pltpu.VMEM((n_space, n) + shape, jnp.float32),
            pltpu.VMEM((n_space, n) + shape, jnp.float32),
            pltpu.VMEM((n,) + shape, jnp.float32),
            pltpu.VMEM((n,) + shape, jnp.float32),
            pltpu.VMEM((n_space * own_lines, size // 2), jnp.float32),
            pltpu.VMEM((n_space,) + shape, jnp.float32),
            pltpu.VMEM((points,), jnp.float32),
            pltpu.SMEM((channels // 2,), jnp.int32),
            pltpu.SemaphoreType.DMA((3, max(4, pairs + 1))),
            pltpu.SemaphoreType.DMA((pairs + 3, n)),
            pltpu.SemaphoreType.DMA((pairs + 3, n)),
            pltpu.SemaphoreType.DMA((2,)),
            pltpu.SemaphoreType.DMA((n_space,)),
            pltpu.SemaphoreType.DMA((n_space,)),
            pltpu.SemaphoreType.DMA((n,)),
            pltpu.SemaphoreType.DMA((n,)),
            pltpu.SemaphoreType.DMA((n_space,)),
            pltpu.SemaphoreType.DMA((n_space,)),
            pltpu.SemaphoreType.REGULAR((n // 2 - 1,)),
        ],
        compiler_params=pltpu.CompilerParams(collective_id=0, has_side_effects=True),
    )(snapshots, closing, weights, bin_index)
    by_pair = sums.reshape(2, own_lines // 2, blocks_all, group // 2)
    return by_pair.transpose(3, 0, 1, 2)


def chosen_body(snapshots, closing, weights, bin_index):
    n, n_space = lax.axis_size("tm"), lax.axis_size("space")
    rows, points = snapshots.shape
    group = 2 * NBINS // n
    blocks_all = n * rows // (NFFT // 2)
    tiles = points // LANES
    fits = (
        2 * NBINS % n == 0
        and n % 2 == 0
        and n_space == 4
        and points % LANES == 0
        and tiles // n % 2 == 1
        and tiles // n > 2
        and tiles % n > 0
        and closing.shape[0] == NFFT // 2
        and rows == NFFT
        and group == 16
        and blocks_all == 16
    )
    return (fused_body if fits else body)(snapshots, closing, weights, bin_index)


def solution(mesh):
    return jax.shard_map(
        chosen_body,
        mesh=mesh,
        in_specs=(P("tm", "space"), P(None, "space"), P("space"), P()),
        out_specs=P("tm", None, "space", None),
        check_vma=False,
    )
```

```python
import functools

import jax
import jax.numpy as jnp
from jax import lax
from jax.experimental import pallas as pl
from jax.experimental.pallas import tpu as pltpu
from jax.sharding import PartitionSpec as P

NFFT = 256
NBINS = 64
LANES = 128
MESH = pl.DeviceIdType.MESH


def passed_along(array, axis, by):
    peers = lax.axis_size(axis)
    pairs = [(i, i + by) for i in range(peers) if 0 <= i + by < peers]
    return lax.ppermute(array, axis, pairs)


def spectral_table(bin_index, length):
    sample = jnp.arange(length, dtype=jnp.int32)
    window = 0.5 - 0.5 * jnp.cos(2.0 * jnp.pi * sample.astype(jnp.float32) / length)
    phase_turns = sample[:, None] * bin_index[None, :] % length
    phase_angle = 2.0 * jnp.pi * phase_turns.astype(jnp.float32) / length
    paired = jnp.stack(
        [window[:, None] * jnp.cos(phase_angle), -window[:, None] * jnp.sin(phase_angle)], axis=2
    )
    return paired.reshape(length, 2 * bin_index.shape[0])


def cross_spectra(first_set, second_set):
    products = jnp.einsum(
        "kaip,kbjp->kabij", first_set, second_set, precision=lax.Precision.HIGHEST
    )
    real_part = products[:, 0, 0] + products[:, 1, 1]
    imag_part = products[:, 0, 1] - products[:, 1, 0]
    return jnp.stack([real_part, imag_part], axis=1)


def body(snapshots, closing, weights, bin_index):
    stride_rows = NFFT // 2
    tail_rows = closing.shape[0]
    blocks_here = snapshots.shape[0] // stride_rows
    points = snapshots.shape[1]
    width_tm = lax.axis_size("tm")
    width_space = lax.axis_size("space")
    blocks_all = blocks_here * width_tm
    own_rows = blocks_all // width_space
    basis_table = spectral_table(bin_index, NFFT)
    incoming = passed_along(snapshots[:tail_rows], "tm", -1)
    last_device = lax.axis_index("tm") == width_tm - 1
    series = jnp.concatenate([snapshots, jnp.where(last_device, closing, incoming)], axis=0)
    leading = series[: blocks_here * stride_rows].reshape(blocks_here, stride_rows, points)
    trailing = series[stride_rows:].reshape(blocks_here, stride_rows, points)
    pieces = jnp.concatenate([leading, trailing], axis=1)
    spectrum = jnp.einsum("nc,bnp->cbp", basis_table, pieces, precision=lax.Precision.HIGHEST)
    spectrum = spectrum.reshape(NBINS, 2, blocks_here, points)
    gathered = lax.all_to_all(spectrum, "tm", split_axis=0, concat_axis=2, tiled=True)
    weighted = gathered * weights
    summed = lax.psum_scatter(
        cross_spectra(gathered, weighted).transpose(2, 0, 1, 3),
        "space",
        scatter_dimension=0,
        tiled=True,
    )
    row_ids = lax.axis_index("space") * own_rows + jnp.arange(own_rows, dtype=jnp.int32)
    diagonal = (row_ids[:, None] == jnp.arange(blocks_all, dtype=jnp.int32)[None, :]).astype(
        jnp.float32
    )
    local_trace = jnp.einsum(
        "rkj,rj->k", summed[:, :, 0, :], diagonal, precision=lax.Precision.HIGHEST
    )
    energy = lax.psum(local_trace, "space")
    spectra = summed * (blocks_all / energy)[None, :, None, None]
    return spectra.transpose(1, 2, 0, 3)


def tile_start(device, tiles, width_tm, space):
    return (device * tiles + (space % 2) * (width_tm // 2)) // width_tm


def halves(value):
    high = value.astype(jnp.bfloat16)
    return high, (value - high.astype(jnp.float32)).astype(jnp.bfloat16)


def matmul(a, b):
    return lax.dot_general(a, b, (((1,), (0,)), ((), ())), preferred_element_type=jnp.float32)


def matmul_nt(a, b):
    return lax.dot_general(a, b, (((1,), (1,)), ((), ())), preferred_element_type=jnp.float32)


def picked(selector, values):
    high, low = halves(values)
    return matmul(selector, high) + matmul(selector, low)


def picked_right(values, selector):
    high, low = halves(values)
    return matmul(high, selector) + matmul(low, selector)


def table_rows(bins, length):
    shape = (bins.shape[0], length)
    sample = lax.broadcasted_iota(jnp.int32, shape, 1)
    odd = (lax.broadcasted_iota(jnp.int32, shape, 0) & 1) == 1
    window = 0.5 - 0.5 * jnp.cos(2.0 * jnp.pi * sample.astype(jnp.float32) / length)
    turns = (sample * bins) & (length - 1)
    angle = 2.0 * jnp.pi * turns.astype(jnp.float32) / length
    return window * jnp.where(odd, -jnp.sin(angle), jnp.cos(angle))


def selections(blocks, group, width_space):
    own = blocks // width_space
    size = blocks * group
    line = lax.broadcasted_iota(jnp.int32, (4 * blocks, size), 0)
    lane = lax.broadcasted_iota(jnp.int32, (4 * blocks, size), 1)
    second = line >= 2 * blocks
    row = line & (2 * blocks - 1)
    imag = (row // own) & 1
    match = row // (2 * own) * own + (row & (own - 1)) == lane // group
    wanted = jnp.where(second, 1 - imag, imag)
    sign = jnp.where((imag == 1) & ~second, -1.0, 1.0)
    left = jnp.where(match & ((lane & 1) == wanted), sign, 0.0)
    line = lax.broadcasted_iota(jnp.int32, (size, blocks * group // 2), 0)
    lane = lax.broadcasted_iota(jnp.int32, (size, blocks * group // 2), 1)
    place = (line // group == lane & (blocks - 1)) & ((line & (group - 1)) // 2 == lane // blocks)
    even = jnp.where(place & ((line & 1) == 0), 1.0, 0.0)
    odd = jnp.where(place & ((line & 1) == 1), 1.0, 0.0)
    return [m.astype(jnp.bfloat16) for m in (left, even, odd)]


def over_blocks(row, blocks):
    lane = lax.broadcasted_iota(jnp.int32, row.shape, 1)
    width = row.shape[1]
    shift = blocks // 2
    while shift > 0:
        up = pltpu.roll(row, shift, 1)
        down = pltpu.roll(row, width - shift, 1)
        row = row + jnp.where((lane & shift) == 0, down, up)
        shift //= 2
    return row


def kernel(
    n,
    n_space,
    snap_ref,
    closing_ref,
    weights_ref,
    bins_ref,
    out_ref,
    series,
    table_ref,
    left_ref,
    even_ref,
    odd_ref,
    a_high,
    a_low,
    b_high,
    b_low,
    gram,
    final,
    part,
    rows_in,
    weights,
    bins,
    local_sem,
    send_sem,
    recv_sem,
    part_send,
    part_recv,
    round_sem,
):
    me = lax.axis_index("tm")
    here = lax.axis_index("space")
    rows, points = snap_ref.shape
    tail_rows = closing_ref.shape[0]
    tiles = points // LANES
    steps = series.shape[0]
    pairs = steps - 1
    hop = NFFT // 2
    blocks_all = n * rows // hop
    channels = 2 * bins_ref.shape[0]
    group = channels // n
    own_rows = blocks_all // n_space

    deep = n // 2
    z, x = me // 2, lax.rem(me, 2)
    near = me // deep * deep
    far = deep - near

    def peer_of(k):
        return lax.rem(me + k, n)

    def begin(device):
        return tile_start(device, tiles, n, here)

    my_start = begin(me)
    my_last = begin(me + 1) - my_start == 2 * steps

    def rows_of(device):
        return pl.ds(pl.multiple_of(device * rows, rows), rows)

    def columns(start, count):
        return pl.ds(pl.multiple_of(start * LANES, LANES), count * LANES)

    def pair_copy(step, peer, sender):
        return pltpu.make_async_remote_copy(
            src_ref=snap_ref.at[:, columns(begin(peer) + 2 * step, 2)],
            dst_ref=series.at[step, rows_of(sender)],
            send_sem=send_sem.at[step, peer],
            recv_sem=recv_sem.at[step, sender],
            device_id={"tm": peer},
            device_id_type=MESH,
        )

    def half_copy(half, peer, sender):
        return pltpu.make_async_remote_copy(
            src_ref=snap_ref.at[:, columns(begin(peer) + 2 * pairs + half, 1)],
            dst_ref=series.at[pairs, rows_of(sender), pl.ds(half * LANES, LANES)],
            send_sem=send_sem.at[pairs + half, peer],
            recv_sem=recv_sem.at[pairs + half, sender],
            device_id={"tm": peer},
            device_id_type=MESH,
        )

    def has_last(device):
        return begin(device + 1) - begin(device) == 2 * steps

    def own_pair(step):
        source = columns(my_start + 2 * step, 2)
        return (
            pltpu.make_async_copy(
                snap_ref.at[:, source], series.at[step, rows_of(me)], local_sem.at[0, step]
            ),
            pltpu.make_async_copy(
                closing_ref.at[:, source],
                series.at[step, pl.ds(n * rows, tail_rows)],
                local_sem.at[1, step],
            ),
        )

    def own_half(half):
        source = columns(my_start + 2 * pairs + half, 1)
        lanes = pl.ds(half * LANES, LANES)
        return (
            pltpu.make_async_copy(
                snap_ref.at[:, source],
                series.at[pairs, rows_of(me), lanes],
                local_sem.at[0, pairs + half],
            ),
            pltpu.make_async_copy(
                closing_ref.at[:, source],
                series.at[pairs, pl.ds(n * rows, tail_rows), lanes],
                local_sem.at[1, pairs + half],
            ),
        )

    weights_copy = pltpu.make_async_copy(weights_ref, weights, local_sem.at[2, 0])
    bins_copy = pltpu.make_async_copy(bins_ref, bins, local_sem.at[2, 1])

    def greet(sem):
        pl.semaphore_signal(sem, inc=1, device_id={"tm": me + 1 - 2 * x}, device_id_type=MESH)

        @pl.when(z + 1 < deep)
        def _():
            pl.semaphore_signal(sem, inc=1, device_id={"tm": me + 2}, device_id_type=MESH)

        @pl.when(z > 0)
        def _():
            pl.semaphore_signal(sem, inc=1, device_id={"tm": me - 2}, device_id_type=MESH)

        for other in (here + 1 - 2 * lax.rem(here, 2), lax.rem(here + 2, n_space)):
            pl.semaphore_signal(sem, inc=1, device_id={"space": other}, device_id_type=MESH)
        pl.semaphore_wait(sem, 3 + (z + 1 < deep).astype(jnp.int32) + (z > 0).astype(jnp.int32))

    def hops(peer):
        return jnp.abs(peer // 2 - z) + jnp.abs(lax.rem(peer, 2) - x)

    for reach in range(1, deep + 1):
        greet(pltpu.get_barrier_semaphore() if reach == 1 else round_sem.at[reach - 2])
        for k in range(1, n):
            peer = peer_of(k)

            @pl.when(hops(peer) == reach)
            def _(peer=peer):
                pair_copy(0, peer, me).start()

    @pl.loop(1, pairs)
    def _(step):
        for k in range(1, n):
            pair_copy(step, peer_of(k), me).start()

    for k in range(1, n):
        half_copy(0, peer_of(k), me).start()
    for k in range(1, n):

        @pl.when(has_last(peer_of(k)))
        def _(k=k):
            half_copy(1, peer_of(k), me).start()

    @pl.loop(0, pairs)
    def _(step):
        for copy in own_pair(step):
            copy.start()

    for copy in own_half(0):
        copy.start()

    @pl.when(my_last)
    def _():
        for copy in own_half(1):
            copy.start()

    weights_copy.start()
    bins_copy.start()
    for reach in range(deep + 1, deep + 3):
        greet(round_sem.at[reach - 2])

    gram[...] = jnp.zeros(gram.shape, jnp.float32)
    left_ref[...], even_ref[...], odd_ref[...] = selections(blocks_all, group, n_space)
    bins_copy.wait()
    channel = lax.broadcasted_iota(jnp.int32, (channels, 1), 0)
    held = jnp.zeros((channels, 1), jnp.int32)
    for k in range(channels // 2):
        held = jnp.where(channel // 2 == k, bins[k], held)
    table_high, table_low = halves(table_rows(held, NFFT))
    table_ref[:channels] = table_high
    table_ref[channels:] = table_low
    weights_copy.wait()

    def transform(step, lanes, weight, half=False):
        def run(turn, carry):
            block = lax.rem(near * (rows // hop) + turn, blocks_all)
            window = pl.ds(pl.multiple_of(block * hop, hop), NFFT)
            high, low = halves(series[step, window, lanes])
            both = matmul(table_ref[...], high)
            coef = both[:channels] + both[channels:] + matmul(table_ref[:channels], low)
            first_high, first_low = halves(coef)
            second_high, second_low = halves(coef * weight)
            place = pl.ds(pl.multiple_of(block * group, group), group)
            for g in range(n):
                cut = slice(g * group, (g + 1) * group)
                if half:
                    a_high[g, place, :LANES] = first_high[cut]
                    a_high[g, place, LANES:] = first_low[cut]
                    b_high[g, place, :LANES] = second_high[cut]
                    b_low[g, place, :LANES] = second_low[cut]
                else:
                    a_high[g, place, :] = first_high[cut]
                    a_low[g, place, :] = first_low[cut]
                    b_high[g, place, :] = second_high[cut]
                    b_low[g, place, :] = second_low[cut]
            return carry

        return run

    def products(g, carry):
        gram[g] += (
            matmul_nt(b_high[g], a_high[g])
            + matmul_nt(b_high[g], a_low[g])
            + matmul_nt(b_low[g], a_high[g])
        )
        return carry

    def half_product(g):
        first, second = a_high[g], b_high[g, :, :LANES]
        return matmul_nt(jnp.concatenate([second, second], axis=1), first) + matmul_nt(
            b_low[g, :, :LANES], first[:, :LANES]
        )

    ready = blocks_all // 2 - 1

    def near_peer(k):
        return near + lax.rem(me - near + k, deep)

    @pl.loop(0, pairs)
    def _(step):
        weight = weights[pl.ds(pl.multiple_of((my_start + 2 * step) * LANES, LANES), 2 * LANES)]
        run = transform(step, slice(0, 2 * LANES), weight.reshape(1, 2 * LANES))
        for copy in own_pair(step):
            copy.wait()
        for k in range(1, deep):
            pair_copy(step, me, near_peer(k)).wait_recv()
        lax.fori_loop(0, ready, run, 0, unroll=ready)
        for k in range(deep):
            pair_copy(step, me, far + k).wait_recv()
        lax.fori_loop(ready, blocks_all, run, 0, unroll=3)
        lax.fori_loop(0, n, products, 0, unroll=2)

    def last(half):
        lanes = slice(half * LANES, (half + 1) * LANES)
        tile = my_start + 2 * pairs + half
        weight = weights[pl.ds(pl.multiple_of(tile * LANES, LANES), LANES)]
        run = transform(pairs, lanes, weight.reshape(1, LANES), half=True)
        for copy in own_half(half):
            copy.wait()
        for k in range(1, deep):
            half_copy(half, me, near_peer(k)).wait_recv()
        lax.fori_loop(0, ready, run, 0, unroll=ready)
        for k in range(deep):
            half_copy(half, me, far + k).wait_recv()
            stop = blocks_all if k == deep - 1 else ready + 2 + 2 * k
            first = ready + 2 * k
            lax.fori_loop(first, stop, run, 0, unroll=stop - first)

    last(0)

    def half_products(g, carry):
        gram[g] += half_product(g)
        return carry

    lax.fori_loop(0, n, half_products, 0, unroll=2)

    size = gram.shape[1]
    row = lax.broadcasted_iota(jnp.int32, (size, size), 0)
    col = lax.broadcasted_iota(jnp.int32, (size, size), 1)
    same_bin = ((row & (group - 1)) >> 1) == ((col & (group - 1)) >> 1)
    line = lax.broadcasted_iota(jnp.int32, part.shape[1:], 0)
    lane = lax.broadcasted_iota(jnp.int32, part.shape[1:], 1)
    imag_row = ((line // own_rows) & 1) == 1
    held_row = line // (2 * own_rows) * own_rows + (line & (own_rows - 1))
    on_diagonal = held_row == lane & (blocks_all - 1)

    def fold(k):
        kept = picked(left_ref[...], jnp.where(same_bin, final[k], 0.0))
        middle = kept.shape[0] // 2
        sums = picked_right(kept[:middle], even_ref[...]) + picked_right(
            kept[middle:], odd_ref[...]
        )
        real = jnp.where(on_diagonal & ~imag_row, sums, 0.0)
        trace = over_blocks(jnp.sum(real, axis=0, keepdims=True), blocks_all)
        part[k] = jnp.where(on_diagonal & imag_row, trace, sums)

    @pl.when(my_last)
    def _():
        last(1)

    def finish(k, g):
        final[k] = gram[g] + jnp.where(my_last, half_product(g), 0.0)

    own_lines = 2 * own_rows

    def part_copy(k, peer, there, sender, sender_space):
        return pltpu.make_async_remote_copy(
            src_ref=part.at[k, pl.ds(there * own_lines, own_lines)],
            dst_ref=rows_in.at[sender, sender_space],
            send_sem=part_send.at[k, there],
            recv_sem=part_recv.at[sender, sender_space],
            device_id={"tm": peer, "space": there},
            device_id_type=MESH,
        )

    def part_arrival(sender, sender_space):
        return part_copy(0, sender, 0, sender, sender_space)

    for k in range(deep):
        finish(k, far + k)
    for k in range(deep):
        fold(k)
    for k in range(deep):
        finish(deep + k, near + k)
    for k in range(deep):
        for there in range(n_space):
            part_copy(k, far + k, there, me, here).start()
    for k in range(deep, n):
        fold(k)
    for k in range(deep):
        for there in range(n_space):

            @pl.when((near + k != me) | (here != there))
            def _(k=k, there=there):
                part_copy(deep + k, near + k, there, me, here).start()

    own = pl.ds(pl.multiple_of(here * own_lines, own_lines), own_lines)
    rows_in[me, here] = part[deep + me - near, own]
    for k in range(deep):
        for there in range(n_space):

            @pl.when((near + k != me) | (here != there))
            def _(k=k, there=there):
                part_arrival(near + k, there).wait_recv()

    for k in range(deep):
        for there in range(n_space):
            part_arrival(far + k, there).wait_recv()
    total = rows_in[0, 0]
    for p in range(n):
        for q in range(n_space):
            if p + q > 0:
                total = total + rows_in[p, q]
    line = lax.broadcasted_iota(jnp.int32, total.shape, 0)
    block = lax.broadcasted_iota(jnp.int32, total.shape, 1) & (blocks_all - 1)
    first = (line == own_rows) & (block == here * own_rows)
    held = jnp.sum(jnp.where(first, total, 0.0), axis=0, keepdims=True)
    energy = over_blocks(held, blocks_all)
    zero = (line >= own_rows) & (block == here * own_rows + (line & (own_rows - 1)))
    spectra = jnp.where(zero, 0.0, total) * (blocks_all / energy)
    for b in range(group // 2):
        out_ref[b] = spectra[:, b * blocks_all : (b + 1) * blocks_all].reshape(out_ref.shape[1:])

    @pl.loop(0, pairs)
    def _(step):
        for k in range(1, n):
            pair_copy(step, peer_of(k), me).wait_send()

    for k in range(1, n):
        half_copy(0, peer_of(k), me).wait_send()

        @pl.when(has_last(peer_of(k)))
        def _(k=k):
            half_copy(1, peer_of(k), me).wait_send()

    for k in range(deep):
        for there in range(n_space):
            part_copy(k, far + k, there, me, here).wait_send()

            @pl.when((near + k != me) | (here != there))
            def _(k=k, there=there):
                part_copy(deep + k, near + k, there, me, here).wait_send()


def fused_body(snapshots, closing, weights, bin_index):
    n, n_space = lax.axis_size("tm"), lax.axis_size("space")
    rows, points = snapshots.shape
    tail_rows = closing.shape[0]
    tiles = points // LANES
    steps = -(-tiles // n) // 2
    blocks_all = n * rows // (NFFT // 2)
    channels = 2 * bin_index.shape[0]
    group = channels // n
    size = blocks_all * group
    own_rows = blocks_all // n_space
    shape = (2 * own_rows, size // 2)
    return pl.pallas_call(
        functools.partial(kernel, n, n_space),
        out_shape=jax.ShapeDtypeStruct((group // 2, 2, own_rows, blocks_all), jnp.float32),
        in_specs=[pl.BlockSpec(memory_space=pl.ANY)] * 4,
        out_specs=pl.BlockSpec(memory_space=pltpu.VMEM),
        scratch_shapes=[
            pltpu.VMEM((steps, n * rows + tail_rows, 2 * LANES), jnp.float32),
            pltpu.VMEM((2 * channels, NFFT), jnp.bfloat16),
            pltpu.VMEM((4 * blocks_all, size), jnp.bfloat16),
            pltpu.VMEM((size, size // 2), jnp.bfloat16),
            pltpu.VMEM((size, size // 2), jnp.bfloat16),
        ]
        + [pltpu.VMEM((n, size, 2 * LANES), jnp.bfloat16)] * 4
        + [
            pltpu.VMEM((n, size, size), jnp.float32),
            pltpu.VMEM((n, size, size), jnp.float32),
            pltpu.VMEM((n, 2 * blocks_all, size // 2), jnp.float32),
            pltpu.VMEM((n, n_space) + shape, jnp.float32),
            pltpu.VMEM((points,), jnp.float32),
            pltpu.SMEM((channels // 2,), jnp.int32),
            pltpu.SemaphoreType.DMA((3, steps + 1)),
            pltpu.SemaphoreType.DMA((steps + 1, n)),
            pltpu.SemaphoreType.DMA((steps + 1, n)),
            pltpu.SemaphoreType.DMA((n, n_space)),
            pltpu.SemaphoreType.DMA((n, n_space)),
            pltpu.SemaphoreType.REGULAR((n // 2 + 1,)),
        ],
        compiler_params=pltpu.CompilerParams(collective_id=0, has_side_effects=True),
    )(snapshots, closing, weights, bin_index)


def chosen_body(snapshots, closing, weights, bin_index):
    n, n_space = lax.axis_size("tm"), lax.axis_size("space")
    rows, points = snapshots.shape
    group = 2 * NBINS // n
    blocks_all = n * rows // (NFFT // 2)
    tiles = points // LANES
    slots = -(-tiles // n)
    fits = (
        2 * NBINS % n == 0
        and n % 2 == 0
        and n_space == 4
        and points % LANES == 0
        and slots % 2 == 0
        and slots > 2
        and tiles // n >= slots - 1
        and closing.shape[0] == NFFT // 2
        and rows == NFFT
        and group == 16
        and blocks_all == 16
    )
    return (fused_body if fits else body)(snapshots, closing, weights, bin_index)


def solution(mesh):
    return jax.shard_map(
        chosen_body,
        mesh=mesh,
        in_specs=(P("tm", "space"), P(None, "space"), P("space"), P()),
        out_specs=P("tm", None, "space", None),
        check_vma=False,
    )
```

```python
import functools

import jax
import jax.numpy as jnp
from jax import lax
from jax.experimental import pallas as pl
from jax.experimental.pallas import tpu as pltpu
from jax.sharding import PartitionSpec as P

NFFT = 256
NBINS = 64
LANES = 128
MESH = pl.DeviceIdType.MESH


def passed_along(array, axis, by):
    peers = lax.axis_size(axis)
    pairs = [(i, i + by) for i in range(peers) if 0 <= i + by < peers]
    return lax.ppermute(array, axis, pairs)


def spectral_table(bin_index, length):
    sample = jnp.arange(length, dtype=jnp.int32)
    window = 0.5 - 0.5 * jnp.cos(2.0 * jnp.pi * sample.astype(jnp.float32) / length)
    phase_turns = sample[:, None] * bin_index[None, :] % length
    phase_angle = 2.0 * jnp.pi * phase_turns.astype(jnp.float32) / length
    paired = jnp.stack(
        [window[:, None] * jnp.cos(phase_angle), -window[:, None] * jnp.sin(phase_angle)], axis=2
    )
    return paired.reshape(length, 2 * bin_index.shape[0])


def cross_spectra(first_set, second_set):
    products = jnp.einsum(
        "kaip,kbjp->kabij", first_set, second_set, precision=lax.Precision.HIGHEST
    )
    real_part = products[:, 0, 0] + products[:, 1, 1]
    imag_part = products[:, 0, 1] - products[:, 1, 0]
    return jnp.stack([real_part, imag_part], axis=1)


def body(snapshots, closing, weights, bin_index):
    stride_rows = NFFT // 2
    tail_rows = closing.shape[0]
    blocks_here = snapshots.shape[0] // stride_rows
    points = snapshots.shape[1]
    width_tm = lax.axis_size("tm")
    width_space = lax.axis_size("space")
    blocks_all = blocks_here * width_tm
    own_rows = blocks_all // width_space
    basis_table = spectral_table(bin_index, NFFT)
    incoming = passed_along(snapshots[:tail_rows], "tm", -1)
    last_device = lax.axis_index("tm") == width_tm - 1
    series = jnp.concatenate([snapshots, jnp.where(last_device, closing, incoming)], axis=0)
    leading = series[: blocks_here * stride_rows].reshape(blocks_here, stride_rows, points)
    trailing = series[stride_rows:].reshape(blocks_here, stride_rows, points)
    pieces = jnp.concatenate([leading, trailing], axis=1)
    spectrum = jnp.einsum("nc,bnp->cbp", basis_table, pieces, precision=lax.Precision.HIGHEST)
    spectrum = spectrum.reshape(NBINS, 2, blocks_here, points)
    gathered = lax.all_to_all(spectrum, "tm", split_axis=0, concat_axis=2, tiled=True)
    weighted = gathered * weights
    summed = lax.psum_scatter(
        cross_spectra(gathered, weighted).transpose(2, 0, 1, 3),
        "space",
        scatter_dimension=0,
        tiled=True,
    )
    row_ids = lax.axis_index("space") * own_rows + jnp.arange(own_rows, dtype=jnp.int32)
    diagonal = (row_ids[:, None] == jnp.arange(blocks_all, dtype=jnp.int32)[None, :]).astype(
        jnp.float32
    )
    local_trace = jnp.einsum(
        "rkj,rj->k", summed[:, :, 0, :], diagonal, precision=lax.Precision.HIGHEST
    )
    energy = lax.psum(local_trace, "space")
    spectra = summed * (blocks_all / energy)[None, :, None, None]
    return spectra.transpose(1, 2, 0, 3)


def tile_start(device, tiles, width_tm, space):
    return (device * tiles + (space % 2) * (width_tm // 2)) // width_tm


def halves(value):
    high = value.astype(jnp.bfloat16)
    return high, (value - high.astype(jnp.float32)).astype(jnp.bfloat16)


def matmul(a, b):
    return lax.dot_general(a, b, (((1,), (0,)), ((), ())), preferred_element_type=jnp.float32)


def matmul_nt(a, b):
    return lax.dot_general(a, b, (((1,), (1,)), ((), ())), preferred_element_type=jnp.float32)


def picked(selector, values):
    high, low = halves(values)
    return matmul(selector, high) + matmul(selector, low)


def picked_right(values, selector):
    high, low = halves(values)
    return matmul(high, selector) + matmul(low, selector)


def table_rows(bins, length):
    shape = (bins.shape[0], length)
    sample = lax.broadcasted_iota(jnp.int32, shape, 1)
    odd = (lax.broadcasted_iota(jnp.int32, shape, 0) & 1) == 1
    window = 0.5 - 0.5 * jnp.cos(2.0 * jnp.pi * sample.astype(jnp.float32) / length)
    turns = (sample * bins) & (length - 1)
    angle = 2.0 * jnp.pi * turns.astype(jnp.float32) / length
    return window * jnp.where(odd, -jnp.sin(angle), jnp.cos(angle))


def selections(blocks, group, width_space):
    own = blocks // width_space
    size = blocks * group
    line = lax.broadcasted_iota(jnp.int32, (4 * blocks, size), 0)
    lane = lax.broadcasted_iota(jnp.int32, (4 * blocks, size), 1)
    second = line >= 2 * blocks
    row = line & (2 * blocks - 1)
    imag = (row // own) & 1
    match = row // (2 * own) * own + (row & (own - 1)) == lane // group
    wanted = jnp.where(second, 1 - imag, imag)
    sign = jnp.where((imag == 1) & ~second, -1.0, 1.0)
    left = jnp.where(match & ((lane & 1) == wanted), sign, 0.0)
    line = lax.broadcasted_iota(jnp.int32, (size, blocks * group // 2), 0)
    lane = lax.broadcasted_iota(jnp.int32, (size, blocks * group // 2), 1)
    place = (line // group == lane & (blocks - 1)) & ((line & (group - 1)) // 2 == lane // blocks)
    even = jnp.where(place & ((line & 1) == 0), 1.0, 0.0)
    odd = jnp.where(place & ((line & 1) == 1), 1.0, 0.0)
    return [m.astype(jnp.bfloat16) for m in (left, even, odd)]


def over_blocks(row, blocks):
    lane = lax.broadcasted_iota(jnp.int32, row.shape, 1)
    width = row.shape[1]
    shift = blocks // 2
    while shift > 0:
        up = pltpu.roll(row, shift, 1)
        down = pltpu.roll(row, width - shift, 1)
        row = row + jnp.where((lane & shift) == 0, down, up)
        shift //= 2
    return row


def kernel(
    n,
    n_space,
    snap_ref,
    closing_ref,
    weights_ref,
    bins_ref,
    out_ref,
    series,
    table_ref,
    left_ref,
    even_ref,
    odd_ref,
    a_high,
    a_low,
    b_high,
    b_low,
    gram,
    final,
    part,
    rows_in,
    weights,
    bins,
    local_sem,
    send_sem,
    recv_sem,
    part_send,
    part_recv,
    round_sem,
):
    me = lax.axis_index("tm")
    here = lax.axis_index("space")
    rows, points = snap_ref.shape
    tail_rows = closing_ref.shape[0]
    tiles = points // LANES
    steps = series.shape[0]
    pairs = steps - 1
    hop = NFFT // 2
    blocks_all = n * rows // hop
    channels = 2 * bins_ref.shape[0]
    group = channels // n
    own_rows = blocks_all // n_space

    deep = n // 2
    z, x = me // 2, lax.rem(me, 2)
    near = me // deep * deep
    far = deep - near

    def peer_of(k):
        return lax.rem(me + k, n)

    def begin(device):
        return tile_start(device, tiles, n, here)

    my_start = begin(me)
    my_last = begin(me + 1) - my_start == 2 * steps

    def rows_of(device):
        return pl.ds(pl.multiple_of(device * rows, rows), rows)

    def columns(start, count):
        return pl.ds(pl.multiple_of(start * LANES, LANES), count * LANES)

    def pair_copy(step, peer, sender):
        return pltpu.make_async_remote_copy(
            src_ref=snap_ref.at[:, columns(begin(peer) + 2 * step, 2)],
            dst_ref=series.at[step, rows_of(sender)],
            send_sem=send_sem.at[step, peer],
            recv_sem=recv_sem.at[step, sender],
            device_id={"tm": peer},
            device_id_type=MESH,
        )

    def half_copy(half, peer, sender):
        return pltpu.make_async_remote_copy(
            src_ref=snap_ref.at[:, columns(begin(peer) + 2 * pairs + half, 1)],
            dst_ref=series.at[pairs, rows_of(sender), pl.ds(half * LANES, LANES)],
            send_sem=send_sem.at[pairs + half, peer],
            recv_sem=recv_sem.at[pairs + half, sender],
            device_id={"tm": peer},
            device_id_type=MESH,
        )

    def has_last(device):
        return begin(device + 1) - begin(device) == 2 * steps

    def own_pair(step):
        source = columns(my_start + 2 * step, 2)
        return (
            pltpu.make_async_copy(
                snap_ref.at[:, source], series.at[step, rows_of(me)], local_sem.at[0, step]
            ),
            pltpu.make_async_copy(
                closing_ref.at[:, source],
                series.at[step, pl.ds(n * rows, tail_rows)],
                local_sem.at[1, step],
            ),
        )

    def own_half(half):
        source = columns(my_start + 2 * pairs + half, 1)
        lanes = pl.ds(half * LANES, LANES)
        return (
            pltpu.make_async_copy(
                snap_ref.at[:, source],
                series.at[pairs, rows_of(me), lanes],
                local_sem.at[0, pairs + half],
            ),
            pltpu.make_async_copy(
                closing_ref.at[:, source],
                series.at[pairs, pl.ds(n * rows, tail_rows), lanes],
                local_sem.at[1, pairs + half],
            ),
        )

    weights_copy = pltpu.make_async_copy(weights_ref, weights, local_sem.at[2, 0])
    bins_copy = pltpu.make_async_copy(bins_ref, bins, local_sem.at[2, 1])

    def greet(sem):
        pl.semaphore_signal(sem, inc=1, device_id={"tm": me + 1 - 2 * x}, device_id_type=MESH)

        @pl.when(z + 1 < deep)
        def _():
            pl.semaphore_signal(sem, inc=1, device_id={"tm": me + 2}, device_id_type=MESH)

        @pl.when(z > 0)
        def _():
            pl.semaphore_signal(sem, inc=1, device_id={"tm": me - 2}, device_id_type=MESH)

        for other in (here + 1 - 2 * lax.rem(here, 2), lax.rem(here + 2, n_space)):
            pl.semaphore_signal(sem, inc=1, device_id={"space": other}, device_id_type=MESH)
        pl.semaphore_wait(sem, 3 + (z + 1 < deep).astype(jnp.int32) + (z > 0).astype(jnp.int32))

    def hops(peer):
        return jnp.abs(peer // 2 - z) + jnp.abs(lax.rem(peer, 2) - x)

    for reach in range(1, deep + 1):
        greet(pltpu.get_barrier_semaphore() if reach == 1 else round_sem.at[reach - 2])
        for k in range(1, n):
            peer = peer_of(k)

            @pl.when(hops(peer) == reach)
            def _(peer=peer):
                pair_copy(0, peer, me).start()

    @pl.loop(1, pairs)
    def _(step):
        for k in range(1, n):
            pair_copy(step, peer_of(k), me).start()

    for k in range(1, n):
        half_copy(0, peer_of(k), me).start()
    for k in range(1, n):

        @pl.when(has_last(peer_of(k)))
        def _(k=k):
            half_copy(1, peer_of(k), me).start()

    @pl.loop(0, pairs)
    def _(step):
        for copy in own_pair(step):
            copy.start()

    for copy in own_half(0):
        copy.start()

    @pl.when(my_last)
    def _():
        for copy in own_half(1):
            copy.start()

    weights_copy.start()
    bins_copy.start()
    for reach in range(deep + 1, deep + 3):
        greet(round_sem.at[reach - 2])

    gram[...] = jnp.zeros(gram.shape, jnp.float32)
    left_ref[...], even_ref[...], odd_ref[...] = selections(blocks_all, group, n_space)
    bins_copy.wait()
    channel = lax.broadcasted_iota(jnp.int32, (channels, 1), 0)
    held = jnp.zeros((channels, 1), jnp.int32)
    for k in range(channels // 2):
        held = jnp.where(channel // 2 == k, bins[k], held)
    table_high, table_low = halves(table_rows(held, NFFT))
    table_ref[:channels] = table_high
    table_ref[channels:] = table_low
    weights_copy.wait()

    def transform(step, lanes, weight, half=False):
        def run(turn, carry):
            block = lax.rem(near * (rows // hop) + turn, blocks_all)
            window = pl.ds(pl.multiple_of(block * hop, hop), NFFT)
            high, low = halves(series[step, window, lanes])
            both = matmul(table_ref[...], high)
            coef = both[:channels] + both[channels:] + matmul(table_ref[:channels], low)
            first_high, first_low = halves(coef)
            second_high, second_low = halves(coef * weight)
            place = pl.ds(pl.multiple_of(block * group, group), group)
            for g in range(n):
                cut = slice(g * group, (g + 1) * group)
                if half:
                    a_high[g, place, :LANES] = first_high[cut]
                    a_high[g, place, LANES:] = first_low[cut]
                    b_high[g, place, :LANES] = second_high[cut]
                    b_low[g, place, :LANES] = second_low[cut]
                else:
                    a_high[g, place, :] = first_high[cut]
                    a_low[g, place, :] = first_low[cut]
                    b_high[g, place, :] = second_high[cut]
                    b_low[g, place, :] = second_low[cut]
            return carry

        return run

    def products(g, carry):
        gram[g] += (
            matmul_nt(b_high[g], a_high[g])
            + matmul_nt(b_high[g], a_low[g])
            + matmul_nt(b_low[g], a_high[g])
        )
        return carry

    def half_product(g):
        first, second = a_high[g], b_high[g, :, :LANES]
        return matmul_nt(jnp.concatenate([second, second], axis=1), first) + matmul_nt(
            b_low[g, :, :LANES], first[:, :LANES]
        )

    ready = blocks_all // 2 - 1

    def near_peer(k):
        return near + lax.rem(me - near + k, deep)

    @pl.loop(0, pairs)
    def _(step):
        weight = weights[pl.ds(pl.multiple_of((my_start + 2 * step) * LANES, LANES), 2 * LANES)]
        run = transform(step, slice(0, 2 * LANES), weight.reshape(1, 2 * LANES))
        for copy in own_pair(step):
            copy.wait()
        for k in range(1, deep):
            pair_copy(step, me, near_peer(k)).wait_recv()
        lax.fori_loop(0, ready, run, 0, unroll=ready)
        for k in range(deep):
            pair_copy(step, me, far + k).wait_recv()
        lax.fori_loop(ready, blocks_all, run, 0, unroll=3)
        lax.fori_loop(0, n, products, 0, unroll=2)

    def last(half):
        lanes = slice(half * LANES, (half + 1) * LANES)
        tile = my_start + 2 * pairs + half
        weight = weights[pl.ds(pl.multiple_of(tile * LANES, LANES), LANES)]
        run = transform(pairs, lanes, weight.reshape(1, LANES), half=True)
        for copy in own_half(half):
            copy.wait()
        for k in range(1, deep):
            half_copy(half, me, near_peer(k)).wait_recv()
        lax.fori_loop(0, ready, run, 0, unroll=ready)
        for k in range(deep):
            half_copy(half, me, far + k).wait_recv()
            stop = blocks_all if k == deep - 1 else ready + 2 + 2 * k
            first = ready + 2 * k
            lax.fori_loop(first, stop, run, 0, unroll=stop - first)

    last(0)

    def half_products(g, carry):
        gram[g] += half_product(g)
        return carry

    lax.fori_loop(0, n, half_products, 0, unroll=2)

    size = gram.shape[1]
    row = lax.broadcasted_iota(jnp.int32, (size, size), 0)
    col = lax.broadcasted_iota(jnp.int32, (size, size), 1)
    same_bin = ((row & (group - 1)) >> 1) == ((col & (group - 1)) >> 1)
    line = lax.broadcasted_iota(jnp.int32, part.shape[1:], 0)
    lane = lax.broadcasted_iota(jnp.int32, part.shape[1:], 1)
    imag_row = ((line // own_rows) & 1) == 1
    held_row = line // (2 * own_rows) * own_rows + (line & (own_rows - 1))
    on_diagonal = held_row == lane & (blocks_all - 1)

    def fold(k):
        kept = picked(left_ref[...], jnp.where(same_bin, final[k], 0.0))
        middle = kept.shape[0] // 2
        sums = picked_right(kept[:middle], even_ref[...]) + picked_right(
            kept[middle:], odd_ref[...]
        )
        real = jnp.where(on_diagonal & ~imag_row, sums, 0.0)
        trace = over_blocks(jnp.sum(real, axis=0, keepdims=True), blocks_all)
        part[k] = jnp.where(on_diagonal & imag_row, trace, sums)

    @pl.when(my_last)
    def _():
        last(1)

    def finish(k, g):
        final[k] = gram[g] + jnp.where(my_last, half_product(g), 0.0)

    own_lines = 2 * own_rows

    def part_copy(k, peer, there, sender, sender_space):
        return pltpu.make_async_remote_copy(
            src_ref=part.at[k, pl.ds(there * own_lines, own_lines)],
            dst_ref=rows_in.at[sender, sender_space],
            send_sem=part_send.at[k, there],
            recv_sem=part_recv.at[sender, sender_space],
            device_id={"tm": peer, "space": there},
            device_id_type=MESH,
        )

    def part_arrival(sender, sender_space):
        return part_copy(0, sender, 0, sender, sender_space)

    for k in range(deep):
        finish(k, far + k)
    for k in range(deep):
        fold(k)
    for k in range(deep):
        finish(deep + k, near + k)
    for k in range(deep):
        for there in range(n_space):
            part_copy(k, far + k, there, me, here).start()
    for k in range(deep, n):
        fold(k)
    for k in range(deep):
        for there in range(n_space):

            @pl.when((near + k != me) | (here != there))
            def _(k=k, there=there):
                part_copy(deep + k, near + k, there, me, here).start()

    own = pl.ds(pl.multiple_of(here * own_lines, own_lines), own_lines)
    rows_in[me, here] = part[deep + me - near, own]
    for k in range(deep):
        for there in range(n_space):

            @pl.when((near + k != me) | (here != there))
            def _(k=k, there=there):
                part_arrival(near + k, there).wait_recv()

    for k in range(deep):
        for there in range(n_space):
            part_arrival(far + k, there).wait_recv()
    total = rows_in[0, 0]
    for p in range(n):
        for q in range(n_space):
            if p + q > 0:
                total = total + rows_in[p, q]
    line = lax.broadcasted_iota(jnp.int32, total.shape, 0)
    block = lax.broadcasted_iota(jnp.int32, total.shape, 1) & (blocks_all - 1)
    first = (line == own_rows) & (block == here * own_rows)
    held = jnp.sum(jnp.where(first, total, 0.0), axis=0, keepdims=True)
    energy = over_blocks(held, blocks_all)
    zero = (line >= own_rows) & (block == here * own_rows + (line & (own_rows - 1)))
    spectra = jnp.where(zero, 0.0, total) * (blocks_all / energy)
    for b in range(group // 2):
        out_ref[b] = spectra[:, b * blocks_all : (b + 1) * blocks_all].reshape(out_ref.shape[1:])

    @pl.loop(0, pairs)
    def _(step):
        for k in range(1, n):
            pair_copy(step, peer_of(k), me).wait_send()

    for k in range(1, n):
        half_copy(0, peer_of(k), me).wait_send()

        @pl.when(has_last(peer_of(k)))
        def _(k=k):
            half_copy(1, peer_of(k), me).wait_send()

    for k in range(deep):
        for there in range(n_space):
            part_copy(k, far + k, there, me, here).wait_send()

            @pl.when((near + k != me) | (here != there))
            def _(k=k, there=there):
                part_copy(deep + k, near + k, there, me, here).wait_send()


def fused_body(snapshots, closing, weights, bin_index):
    n, n_space = lax.axis_size("tm"), lax.axis_size("space")
    rows, points = snapshots.shape
    tail_rows = closing.shape[0]
    tiles = points // LANES
    steps = -(-tiles // n) // 2
    blocks_all = n * rows // (NFFT // 2)
    channels = 2 * bin_index.shape[0]
    group = channels // n
    size = blocks_all * group
    own_rows = blocks_all // n_space
    shape = (2 * own_rows, size // 2)
    return pl.pallas_call(
        functools.partial(kernel, n, n_space),
        out_shape=pltpu.VMEM((group // 2, 2, own_rows, blocks_all), jnp.float32),
        in_specs=[pl.BlockSpec(memory_space=pl.ANY)] * 4,
        out_specs=pl.BlockSpec(memory_space=pltpu.VMEM),
        scratch_shapes=[
            pltpu.VMEM((steps, n * rows + tail_rows, 2 * LANES), jnp.float32),
            pltpu.VMEM((2 * channels, NFFT), jnp.bfloat16),
            pltpu.VMEM((4 * blocks_all, size), jnp.bfloat16),
            pltpu.VMEM((size, size // 2), jnp.bfloat16),
            pltpu.VMEM((size, size // 2), jnp.bfloat16),
        ]
        + [pltpu.VMEM((n, size, 2 * LANES), jnp.bfloat16)] * 4
        + [
            pltpu.VMEM((n, size, size), jnp.float32),
            pltpu.VMEM((n, size, size), jnp.float32),
            pltpu.VMEM((n, 2 * blocks_all, size // 2), jnp.float32),
            pltpu.VMEM((n, n_space) + shape, jnp.float32),
            pltpu.VMEM((points,), jnp.float32),
            pltpu.SMEM((channels // 2,), jnp.int32),
            pltpu.SemaphoreType.DMA((3, steps + 1)),
            pltpu.SemaphoreType.DMA((steps + 1, n)),
            pltpu.SemaphoreType.DMA((steps + 1, n)),
            pltpu.SemaphoreType.DMA((n, n_space)),
            pltpu.SemaphoreType.DMA((n, n_space)),
            pltpu.SemaphoreType.REGULAR((n // 2 + 1,)),
        ],
        compiler_params=pltpu.CompilerParams(collective_id=0, has_side_effects=True),
    )(snapshots, closing, weights, bin_index)


def chosen_body(snapshots, closing, weights, bin_index):
    n, n_space = lax.axis_size("tm"), lax.axis_size("space")
    rows, points = snapshots.shape
    group = 2 * NBINS // n
    blocks_all = n * rows // (NFFT // 2)
    tiles = points // LANES
    slots = -(-tiles // n)
    fits = (
        2 * NBINS % n == 0
        and n % 2 == 0
        and n_space == 4
        and points % LANES == 0
        and slots % 2 == 0
        and slots > 2
        and tiles // n >= slots - 1
        and closing.shape[0] == NFFT // 2
        and rows == NFFT
        and group == 16
        and blocks_all == 16
    )
    return (fused_body if fits else body)(snapshots, closing, weights, bin_index)


def solution(mesh):
    return jax.shard_map(
        chosen_body,
        mesh=mesh,
        in_specs=(P("tm", "space"), P(None, "space"), P("space"), P()),
        out_specs=P("tm", None, "space", None),
        check_vma=False,
    )
```

```python
import functools

import jax
import jax.numpy as jnp
from jax import lax
from jax.experimental import pallas as pl
from jax.experimental.pallas import tpu as pltpu
from jax.sharding import PartitionSpec as P

NFFT = 256
NBINS = 64
LANES = 128
MESH = pl.DeviceIdType.MESH


def passed_along(array, axis, by):
    peers = lax.axis_size(axis)
    pairs = [(i, i + by) for i in range(peers) if 0 <= i + by < peers]
    return lax.ppermute(array, axis, pairs)


def spectral_table(bin_index, length):
    sample = jnp.arange(length, dtype=jnp.int32)
    window = 0.5 - 0.5 * jnp.cos(2.0 * jnp.pi * sample.astype(jnp.float32) / length)
    phase_turns = sample[:, None] * bin_index[None, :] % length
    phase_angle = 2.0 * jnp.pi * phase_turns.astype(jnp.float32) / length
    paired = jnp.stack(
        [window[:, None] * jnp.cos(phase_angle), -window[:, None] * jnp.sin(phase_angle)], axis=2
    )
    return paired.reshape(length, 2 * bin_index.shape[0])


def cross_spectra(first_set, second_set):
    products = jnp.einsum(
        "kaip,kbjp->kabij", first_set, second_set, precision=lax.Precision.HIGHEST
    )
    real_part = products[:, 0, 0] + products[:, 1, 1]
    imag_part = products[:, 0, 1] - products[:, 1, 0]
    return jnp.stack([real_part, imag_part], axis=1)


def body(snapshots, closing, weights, bin_index):
    stride_rows = NFFT // 2
    tail_rows = closing.shape[0]
    blocks_here = snapshots.shape[0] // stride_rows
    points = snapshots.shape[1]
    width_tm = lax.axis_size("tm")
    width_space = lax.axis_size("space")
    blocks_all = blocks_here * width_tm
    own_rows = blocks_all // width_space
    basis_table = spectral_table(bin_index, NFFT)
    incoming = passed_along(snapshots[:tail_rows], "tm", -1)
    last_device = lax.axis_index("tm") == width_tm - 1
    series = jnp.concatenate([snapshots, jnp.where(last_device, closing, incoming)], axis=0)
    leading = series[: blocks_here * stride_rows].reshape(blocks_here, stride_rows, points)
    trailing = series[stride_rows:].reshape(blocks_here, stride_rows, points)
    pieces = jnp.concatenate([leading, trailing], axis=1)
    spectrum = jnp.einsum("nc,bnp->cbp", basis_table, pieces, precision=lax.Precision.HIGHEST)
    spectrum = spectrum.reshape(NBINS, 2, blocks_here, points)
    gathered = lax.all_to_all(spectrum, "tm", split_axis=0, concat_axis=2, tiled=True)
    weighted = gathered * weights
    summed = lax.psum_scatter(
        cross_spectra(gathered, weighted).transpose(2, 0, 1, 3),
        "space",
        scatter_dimension=0,
        tiled=True,
    )
    row_ids = lax.axis_index("space") * own_rows + jnp.arange(own_rows, dtype=jnp.int32)
    diagonal = (row_ids[:, None] == jnp.arange(blocks_all, dtype=jnp.int32)[None, :]).astype(
        jnp.float32
    )
    local_trace = jnp.einsum(
        "rkj,rj->k", summed[:, :, 0, :], diagonal, precision=lax.Precision.HIGHEST
    )
    energy = lax.psum(local_trace, "space")
    spectra = summed * (blocks_all / energy)[None, :, None, None]
    return spectra.transpose(1, 2, 0, 3)


def tile_start(device, tiles, width_tm, space):
    return (device * tiles + (space % 2) * (width_tm // 2)) // width_tm


def halves(value):
    high = value.astype(jnp.bfloat16)
    return high, (value - high.astype(jnp.float32)).astype(jnp.bfloat16)


def matmul(a, b):
    return lax.dot_general(a, b, (((1,), (0,)), ((), ())), preferred_element_type=jnp.float32)


def matmul_nt(a, b):
    return lax.dot_general(a, b, (((1,), (1,)), ((), ())), preferred_element_type=jnp.float32)


def picked(selector, values):
    high, low = halves(values)
    return matmul(selector, high) + matmul(selector, low)


def picked_right(values, selector):
    high, low = halves(values)
    return matmul(high, selector) + matmul(low, selector)


def table_rows(bins, length):
    shape = (bins.shape[0], length)
    sample = lax.broadcasted_iota(jnp.int32, shape, 1)
    odd = (lax.broadcasted_iota(jnp.int32, shape, 0) & 1) == 1
    window = 0.5 - 0.5 * jnp.cos(2.0 * jnp.pi * sample.astype(jnp.float32) / length)
    turns = (sample * bins) & (length - 1)
    angle = 2.0 * jnp.pi * turns.astype(jnp.float32) / length
    return window * jnp.where(odd, -jnp.sin(angle), jnp.cos(angle))


def selections(blocks, group, width_space):
    own = blocks // width_space
    size = blocks * group
    line = lax.broadcasted_iota(jnp.int32, (4 * blocks, size), 0)
    lane = lax.broadcasted_iota(jnp.int32, (4 * blocks, size), 1)
    second = line >= 2 * blocks
    row = line & (2 * blocks - 1)
    imag = (row // own) & 1
    match = row // (2 * own) * own + (row & (own - 1)) == lane // group
    wanted = jnp.where(second, 1 - imag, imag)
    sign = jnp.where((imag == 1) & ~second, -1.0, 1.0)
    left = jnp.where(match & ((lane & 1) == wanted), sign, 0.0)
    line = lax.broadcasted_iota(jnp.int32, (size, blocks * group // 2), 0)
    lane = lax.broadcasted_iota(jnp.int32, (size, blocks * group // 2), 1)
    place = (line // group == lane & (blocks - 1)) & ((line & (group - 1)) // 2 == lane // blocks)
    even = jnp.where(place & ((line & 1) == 0), 1.0, 0.0)
    odd = jnp.where(place & ((line & 1) == 1), 1.0, 0.0)
    return [m.astype(jnp.bfloat16) for m in (left, even, odd)]


def over_blocks(row, blocks):
    lane = lax.broadcasted_iota(jnp.int32, row.shape, 1)
    width = row.shape[1]
    shift = blocks // 2
    while shift > 0:
        up = pltpu.roll(row, shift, 1)
        down = pltpu.roll(row, width - shift, 1)
        row = row + jnp.where((lane & shift) == 0, down, up)
        shift //= 2
    return row


def kernel(
    n,
    n_space,
    snap_ref,
    closing_ref,
    weights_ref,
    bins_ref,
    out_ref,
    series,
    table_ref,
    left_ref,
    even_ref,
    odd_ref,
    a_high,
    a_low,
    b_high,
    b_low,
    gram,
    final,
    part,
    rows_in,
    weights,
    bins,
    local_sem,
    send_sem,
    recv_sem,
    part_send,
    part_recv,
    round_sem,
):
    me = lax.axis_index("tm")
    here = lax.axis_index("space")
    rows, points = snap_ref.shape
    tail_rows = closing_ref.shape[0]
    tiles = points // LANES
    steps = series.shape[0]
    pairs = steps - 1
    hop = NFFT // 2
    blocks_all = n * rows // hop
    channels = 2 * bins_ref.shape[0]
    group = channels // n
    own_rows = blocks_all // n_space

    deep = n // 2
    z, x = me // 2, lax.rem(me, 2)
    near = me // deep * deep
    far = deep - near

    def peer_of(k):
        return lax.rem(me + k, n)

    def begin(device):
        return tile_start(device, tiles, n, here)

    my_start = begin(me)
    my_last = begin(me + 1) - my_start == 2 * steps

    def rows_of(device):
        return pl.ds(pl.multiple_of(device * rows, rows), rows)

    def columns(start, count):
        return pl.ds(pl.multiple_of(start * LANES, LANES), count * LANES)

    def pair_copy(step, peer, sender):
        return pltpu.make_async_remote_copy(
            src_ref=snap_ref.at[:, columns(begin(peer) + 2 * step, 2)],
            dst_ref=series.at[step, rows_of(sender)],
            send_sem=send_sem.at[step, peer],
            recv_sem=recv_sem.at[step, sender],
            device_id={"tm": peer},
            device_id_type=MESH,
        )

    def half_copy(half, peer, sender):
        return pltpu.make_async_remote_copy(
            src_ref=snap_ref.at[:, columns(begin(peer) + 2 * pairs + half, 1)],
            dst_ref=series.at[pairs, rows_of(sender), pl.ds(half * LANES, LANES)],
            send_sem=send_sem.at[pairs + half, peer],
            recv_sem=recv_sem.at[pairs + half, sender],
            device_id={"tm": peer},
            device_id_type=MESH,
        )

    def has_last(device):
        return begin(device + 1) - begin(device) == 2 * steps

    def own_pair(step):
        source = columns(my_start + 2 * step, 2)
        return (
            pltpu.make_async_copy(
                snap_ref.at[:, source], series.at[step, rows_of(me)], local_sem.at[0, step]
            ),
            pltpu.make_async_copy(
                closing_ref.at[:, source],
                series.at[step, pl.ds(n * rows, tail_rows)],
                local_sem.at[1, step],
            ),
        )

    def own_half(half):
        source = columns(my_start + 2 * pairs + half, 1)
        lanes = pl.ds(half * LANES, LANES)
        return (
            pltpu.make_async_copy(
                snap_ref.at[:, source],
                series.at[pairs, rows_of(me), lanes],
                local_sem.at[0, pairs + half],
            ),
            pltpu.make_async_copy(
                closing_ref.at[:, source],
                series.at[pairs, pl.ds(n * rows, tail_rows), lanes],
                local_sem.at[1, pairs + half],
            ),
        )

    weights_copy = pltpu.make_async_copy(weights_ref, weights, local_sem.at[2, 0])
    bins_copy = pltpu.make_async_copy(bins_ref, bins, local_sem.at[2, 1])

    def greet(sem):
        pl.semaphore_signal(sem, inc=1, device_id={"tm": me + 1 - 2 * x}, device_id_type=MESH)

        @pl.when(z + 1 < deep)
        def _():
            pl.semaphore_signal(sem, inc=1, device_id={"tm": me + 2}, device_id_type=MESH)

        @pl.when(z > 0)
        def _():
            pl.semaphore_signal(sem, inc=1, device_id={"tm": me - 2}, device_id_type=MESH)

        for other in (here + 1 - 2 * lax.rem(here, 2), lax.rem(here + 2, n_space)):
            pl.semaphore_signal(sem, inc=1, device_id={"space": other}, device_id_type=MESH)
        pl.semaphore_wait(sem, 3 + (z + 1 < deep).astype(jnp.int32) + (z > 0).astype(jnp.int32))

    def hops(peer):
        return jnp.abs(peer // 2 - z) + jnp.abs(lax.rem(peer, 2) - x)

    for reach in range(1, deep + 1):
        greet(pltpu.get_barrier_semaphore() if reach == 1 else round_sem.at[reach - 2])
        for k in range(1, n):
            peer = peer_of(k)

            @pl.when(hops(peer) == reach)
            def _(peer=peer):
                pair_copy(0, peer, me).start()

    @pl.loop(1, pairs)
    def _(step):
        for k in [3, 4, 5, 6, 7, 1, 2]:
            pair_copy(step, peer_of(k), me).start()

    for k in [3, 4, 5, 6, 7, 1, 2]:
        half_copy(0, peer_of(k), me).start()
    for k in [3, 4, 5, 6, 7, 1, 2]:

        @pl.when(has_last(peer_of(k)))
        def _(k=k):
            half_copy(1, peer_of(k), me).start()

    @pl.loop(0, pairs)
    def _(step):
        for copy in own_pair(step):
            copy.start()

    for copy in own_half(0):
        copy.start()

    @pl.when(my_last)
    def _():
        for copy in own_half(1):
            copy.start()

    weights_copy.start()
    bins_copy.start()
    for reach in range(deep + 1, deep + 3):
        greet(round_sem.at[reach - 2])

    gram[...] = jnp.zeros(gram.shape, jnp.float32)
    left_ref[...], even_ref[...], odd_ref[...] = selections(blocks_all, group, n_space)
    bins_copy.wait()
    channel = lax.broadcasted_iota(jnp.int32, (channels, 1), 0)
    held = jnp.zeros((channels, 1), jnp.int32)
    for k in range(channels // 2):
        held = jnp.where(channel // 2 == k, bins[k], held)
    table_high, table_low = halves(table_rows(held, NFFT))
    table_ref[:channels] = table_high
    table_ref[channels:] = table_low
    weights_copy.wait()

    def transform(step, lanes, weight, half=False):
        def run(turn, carry):
            block = lax.rem(near * (rows // hop) + turn, blocks_all)
            window = pl.ds(pl.multiple_of(block * hop, hop), NFFT)
            high, low = halves(series[step, window, lanes])
            both = matmul(table_ref[...], high)
            coef = both[:channels] + both[channels:] + matmul(table_ref[:channels], low)
            first_high, first_low = halves(coef)
            second_high, second_low = halves(coef * weight)
            place = pl.ds(pl.multiple_of(block * group, group), group)
            for g in range(n):
                cut = slice(g * group, (g + 1) * group)
                if half:
                    a_high[g, place, :LANES] = first_high[cut]
                    a_high[g, place, LANES:] = first_low[cut]
                    b_high[g, place, :LANES] = second_high[cut]
                    b_low[g, place, :LANES] = second_low[cut]
                else:
                    a_high[g, place, :] = first_high[cut]
                    a_low[g, place, :] = first_low[cut]
                    b_high[g, place, :] = second_high[cut]
                    b_low[g, place, :] = second_low[cut]
            return carry

        return run

    def products(g, carry):
        gram[g] += (
            matmul_nt(b_high[g], a_high[g])
            + matmul_nt(b_high[g], a_low[g])
            + matmul_nt(b_low[g], a_high[g])
        )
        return carry

    def half_product(g):
        first, second = a_high[g], b_high[g, :, :LANES]
        return matmul_nt(jnp.concatenate([second, second], axis=1), first) + matmul_nt(
            b_low[g, :, :LANES], first[:, :LANES]
        )

    ready = blocks_all // 2 - 1

    def near_peer(k):
        return near + lax.rem(me - near + k, deep)

    @pl.loop(0, pairs)
    def _(step):
        weight = weights[pl.ds(pl.multiple_of((my_start + 2 * step) * LANES, LANES), 2 * LANES)]
        run = transform(step, slice(0, 2 * LANES), weight.reshape(1, 2 * LANES))
        for copy in own_pair(step):
            copy.wait()
        for k in range(1, deep):
            pair_copy(step, me, near_peer(k)).wait_recv()
        lax.fori_loop(0, ready, run, 0, unroll=ready)
        for k in range(deep):
            pair_copy(step, me, far + k).wait_recv()
        lax.fori_loop(ready, blocks_all, run, 0, unroll=3)
        lax.fori_loop(0, n, products, 0, unroll=2)

    def last(half):
        lanes = slice(half * LANES, (half + 1) * LANES)
        tile = my_start + 2 * pairs + half
        weight = weights[pl.ds(pl.multiple_of(tile * LANES, LANES), LANES)]
        run = transform(pairs, lanes, weight.reshape(1, LANES), half=True)
        for copy in own_half(half):
            copy.wait()
        for k in range(1, deep):
            half_copy(half, me, near_peer(k)).wait_recv()
        lax.fori_loop(0, ready, run, 0, unroll=ready)
        for k in range(deep):
            half_copy(half, me, far + k).wait_recv()
            stop = blocks_all if k == deep - 1 else ready + 2 + 2 * k
            first = ready + 2 * k
            lax.fori_loop(first, stop, run, 0, unroll=stop - first)

    last(0)

    def half_products(g, carry):
        gram[g] += half_product(g)
        return carry

    lax.fori_loop(0, n, half_products, 0, unroll=2)

    size = gram.shape[1]
    row = lax.broadcasted_iota(jnp.int32, (size, size), 0)
    col = lax.broadcasted_iota(jnp.int32, (size, size), 1)
    same_bin = ((row & (group - 1)) >> 1) == ((col & (group - 1)) >> 1)
    line = lax.broadcasted_iota(jnp.int32, part.shape[1:], 0)
    lane = lax.broadcasted_iota(jnp.int32, part.shape[1:], 1)
    imag_row = ((line // own_rows) & 1) == 1
    held_row = line // (2 * own_rows) * own_rows + (line & (own_rows - 1))
    on_diagonal = held_row == lane & (blocks_all - 1)

    def fold(k):
        kept = picked(left_ref[...], jnp.where(same_bin, final[k], 0.0))
        middle = kept.shape[0] // 2
        sums = picked_right(kept[:middle], even_ref[...]) + picked_right(
            kept[middle:], odd_ref[...]
        )
        real = jnp.where(on_diagonal & ~imag_row, sums, 0.0)
        trace = over_blocks(jnp.sum(real, axis=0, keepdims=True), blocks_all)
        part[k] = jnp.where(on_diagonal & imag_row, trace, sums)

    @pl.when(my_last)
    def _():
        last(1)

    def finish(k, g):
        final[k] = gram[g] + jnp.where(my_last, half_product(g), 0.0)

    own_lines = 2 * own_rows

    def part_copy(k, peer, there, sender, sender_space):
        return pltpu.make_async_remote_copy(
            src_ref=part.at[k, pl.ds(there * own_lines, own_lines)],
            dst_ref=rows_in.at[sender, sender_space],
            send_sem=part_send.at[k, there],
            recv_sem=part_recv.at[sender, sender_space],
            device_id={"tm": peer, "space": there},
            device_id_type=MESH,
        )

    def part_arrival(sender, sender_space):
        return part_copy(0, sender, 0, sender, sender_space)

    for k in range(deep):
        finish(k, far + k)
    for k in range(deep):
        fold(k)
    for k in range(deep):
        finish(deep + k, near + k)
    for k in range(deep):
        for there in range(n_space):
            part_copy(k, far + k, there, me, here).start()
    for k in range(deep, n):
        fold(k)
    for k in range(deep):
        for there in range(n_space):

            @pl.when((near + k != me) | (here != there))
            def _(k=k, there=there):
                part_copy(deep + k, near + k, there, me, here).start()

    @pl.loop(0, pairs)
    def _(step):
        for k in range(1, n):
            pair_copy(step, peer_of(k), me).wait_send()

    for k in range(1, n):
        half_copy(0, peer_of(k), me).wait_send()

        @pl.when(has_last(peer_of(k)))
        def _(k=k):
            half_copy(1, peer_of(k), me).wait_send()

    own = pl.ds(pl.multiple_of(here * own_lines, own_lines), own_lines)
    rows_in[me, here] = part[deep + me - near, own]
    for k in range(deep):
        for there in range(n_space):
            part_copy(k, far + k, there, me, here).wait_send()

            @pl.when((near + k != me) | (here != there))
            def _(k=k, there=there):
                part_copy(deep + k, near + k, there, me, here).wait_send()

    for k in range(deep):
        for there in range(n_space):

            @pl.when((near + k != me) | (here != there))
            def _(k=k, there=there):
                part_arrival(near + k, there).wait_recv()

    for k in range(deep):
        for there in range(n_space):
            part_arrival(far + k, there).wait_recv()
    total = rows_in[0, 0]
    for p in range(n):
        for q in range(n_space):
            if p + q > 0:
                total = total + rows_in[p, q]
    line = lax.broadcasted_iota(jnp.int32, total.shape, 0)
    block = lax.broadcasted_iota(jnp.int32, total.shape, 1) & (blocks_all - 1)
    first = (line == own_rows) & (block == here * own_rows)
    held = jnp.sum(jnp.where(first, total, 0.0), axis=0, keepdims=True)
    energy = over_blocks(held, blocks_all)
    zero = (line >= own_rows) & (block == here * own_rows + (line & (own_rows - 1)))
    spectra = jnp.where(zero, 0.0, total) * (blocks_all / energy)
    for b in range(group // 2):
        out_ref[b] = spectra[:, b * blocks_all : (b + 1) * blocks_all].reshape(out_ref.shape[1:])


def fused_body(snapshots, closing, weights, bin_index):
    n, n_space = lax.axis_size("tm"), lax.axis_size("space")
    rows, points = snapshots.shape
    tail_rows = closing.shape[0]
    tiles = points // LANES
    steps = -(-tiles // n) // 2
    blocks_all = n * rows // (NFFT // 2)
    channels = 2 * bin_index.shape[0]
    group = channels // n
    size = blocks_all * group
    own_rows = blocks_all // n_space
    shape = (2 * own_rows, size // 2)
    return pl.pallas_call(
        functools.partial(kernel, n, n_space),
        out_shape=pltpu.VMEM((group // 2, 2, own_rows, blocks_all), jnp.float32),
        in_specs=[pl.BlockSpec(memory_space=pl.ANY)] * 4,
        out_specs=pl.BlockSpec(memory_space=pltpu.VMEM),
        scratch_shapes=[
            pltpu.VMEM((steps, n * rows + tail_rows, 2 * LANES), jnp.float32),
            pltpu.VMEM((2 * channels, NFFT), jnp.bfloat16),
            pltpu.VMEM((4 * blocks_all, size), jnp.bfloat16),
            pltpu.VMEM((size, size // 2), jnp.bfloat16),
            pltpu.VMEM((size, size // 2), jnp.bfloat16),
        ]
        + [pltpu.VMEM((n, size, 2 * LANES), jnp.bfloat16)] * 4
        + [
            pltpu.VMEM((n, size, size), jnp.float32),
            pltpu.VMEM((n, size, size), jnp.float32),
            pltpu.VMEM((n, 2 * blocks_all, size // 2), jnp.float32),
            pltpu.VMEM((n, n_space) + shape, jnp.float32),
            pltpu.VMEM((points,), jnp.float32),
            pltpu.SMEM((channels // 2,), jnp.int32),
            pltpu.SemaphoreType.DMA((3, steps + 1)),
            pltpu.SemaphoreType.DMA((steps + 1, n)),
            pltpu.SemaphoreType.DMA((steps + 1, n)),
            pltpu.SemaphoreType.DMA((n, n_space)),
            pltpu.SemaphoreType.DMA((n, n_space)),
            pltpu.SemaphoreType.REGULAR((n // 2 + 1,)),
        ],
        compiler_params=pltpu.CompilerParams(collective_id=0, has_side_effects=True),
    )(snapshots, closing, weights, bin_index)


def chosen_body(snapshots, closing, weights, bin_index):
    n, n_space = lax.axis_size("tm"), lax.axis_size("space")
    rows, points = snapshots.shape
    group = 2 * NBINS // n
    blocks_all = n * rows // (NFFT // 2)
    tiles = points // LANES
    slots = -(-tiles // n)
    fits = (
        2 * NBINS % n == 0
        and n % 2 == 0
        and n_space == 4
        and points % LANES == 0
        and slots % 2 == 0
        and slots > 2
        and tiles // n >= slots - 1
        and closing.shape[0] == NFFT // 2
        and rows == NFFT
        and group == 16
        and blocks_all == 16
    )
    return (fused_body if fits else body)(snapshots, closing, weights, bin_index)


def solution(mesh):
    return jax.shard_map(
        chosen_body,
        mesh=mesh,
        in_specs=(P("tm", "space"), P(None, "space"), P("space"), P()),
        out_specs=P("tm", None, "space", None),
        check_vma=False,
    )
```

```python
import functools

import jax
import jax.numpy as jnp
from jax import lax
from jax.experimental import pallas as pl
from jax.experimental.pallas import tpu as pltpu
from jax.sharding import PartitionSpec as P

NFFT = 256
NBINS = 64
LANES = 128
MESH = pl.DeviceIdType.MESH


def passed_along(array, axis, by):
    peers = lax.axis_size(axis)
    pairs = [(i, i + by) for i in range(peers) if 0 <= i + by < peers]
    return lax.ppermute(array, axis, pairs)


def spectral_table(bin_index, length):
    sample = jnp.arange(length, dtype=jnp.int32)
    window = 0.5 - 0.5 * jnp.cos(2.0 * jnp.pi * sample.astype(jnp.float32) / length)
    phase_turns = sample[:, None] * bin_index[None, :] % length
    phase_angle = 2.0 * jnp.pi * phase_turns.astype(jnp.float32) / length
    paired = jnp.stack(
        [window[:, None] * jnp.cos(phase_angle), -window[:, None] * jnp.sin(phase_angle)], axis=2
    )
    return paired.reshape(length, 2 * bin_index.shape[0])


def cross_spectra(first_set, second_set):
    products = jnp.einsum(
        "kaip,kbjp->kabij", first_set, second_set, precision=lax.Precision.HIGHEST
    )
    real_part = products[:, 0, 0] + products[:, 1, 1]
    imag_part = products[:, 0, 1] - products[:, 1, 0]
    return jnp.stack([real_part, imag_part], axis=1)


def body(snapshots, closing, weights, bin_index):
    stride_rows = NFFT // 2
    tail_rows = closing.shape[0]
    blocks_here = snapshots.shape[0] // stride_rows
    points = snapshots.shape[1]
    width_tm = lax.axis_size("tm")
    width_space = lax.axis_size("space")
    blocks_all = blocks_here * width_tm
    own_rows = blocks_all // width_space
    basis_table = spectral_table(bin_index, NFFT)
    incoming = passed_along(snapshots[:tail_rows], "tm", -1)
    last_device = lax.axis_index("tm") == width_tm - 1
    series = jnp.concatenate([snapshots, jnp.where(last_device, closing, incoming)], axis=0)
    leading = series[: blocks_here * stride_rows].reshape(blocks_here, stride_rows, points)
    trailing = series[stride_rows:].reshape(blocks_here, stride_rows, points)
    pieces = jnp.concatenate([leading, trailing], axis=1)
    spectrum = jnp.einsum("nc,bnp->cbp", basis_table, pieces, precision=lax.Precision.HIGHEST)
    spectrum = spectrum.reshape(NBINS, 2, blocks_here, points)
    gathered = lax.all_to_all(spectrum, "tm", split_axis=0, concat_axis=2, tiled=True)
    weighted = gathered * weights
    summed = lax.psum_scatter(
        cross_spectra(gathered, weighted).transpose(2, 0, 1, 3),
        "space",
        scatter_dimension=0,
        tiled=True,
    )
    row_ids = lax.axis_index("space") * own_rows + jnp.arange(own_rows, dtype=jnp.int32)
    diagonal = (row_ids[:, None] == jnp.arange(blocks_all, dtype=jnp.int32)[None, :]).astype(
        jnp.float32
    )
    local_trace = jnp.einsum(
        "rkj,rj->k", summed[:, :, 0, :], diagonal, precision=lax.Precision.HIGHEST
    )
    energy = lax.psum(local_trace, "space")
    spectra = summed * (blocks_all / energy)[None, :, None, None]
    return spectra.transpose(1, 2, 0, 3)


def tile_start(device, tiles, width_tm, space):
    return (device * tiles + (space % 2) * (width_tm // 2)) // width_tm


def halves(value):
    high = value.astype(jnp.bfloat16)
    return high, (value - high.astype(jnp.float32)).astype(jnp.bfloat16)


def matmul(a, b):
    return lax.dot_general(a, b, (((1,), (0,)), ((), ())), preferred_element_type=jnp.float32)


def matmul_nt(a, b):
    return lax.dot_general(a, b, (((1,), (1,)), ((), ())), preferred_element_type=jnp.float32)


def picked(selector, values):
    high, low = halves(values)
    return matmul(selector, high) + matmul(selector, low)


def picked_right(values, selector):
    high, low = halves(values)
    return matmul(high, selector) + matmul(low, selector)


def table_rows(bins, length):
    shape = (bins.shape[0], length)
    sample = lax.broadcasted_iota(jnp.int32, shape, 1)
    odd = (lax.broadcasted_iota(jnp.int32, shape, 0) & 1) == 1
    window = 0.5 - 0.5 * jnp.cos(2.0 * jnp.pi * sample.astype(jnp.float32) / length)
    turns = (sample * bins) & (length - 1)
    angle = 2.0 * jnp.pi * turns.astype(jnp.float32) / length
    return window * jnp.where(odd, -jnp.sin(angle), jnp.cos(angle))


def selections(blocks, group, width_space):
    own = blocks // width_space
    size = blocks * group
    line = lax.broadcasted_iota(jnp.int32, (4 * blocks, size), 0)
    lane = lax.broadcasted_iota(jnp.int32, (4 * blocks, size), 1)
    second = line >= 2 * blocks
    row = line & (2 * blocks - 1)
    imag = (row // own) & 1
    match = row // (2 * own) * own + (row & (own - 1)) == lane // group
    wanted = jnp.where(second, 1 - imag, imag)
    sign = jnp.where((imag == 1) & ~second, -1.0, 1.0)
    left = jnp.where(match & ((lane & 1) == wanted), sign, 0.0)
    line = lax.broadcasted_iota(jnp.int32, (size, blocks * group // 2), 0)
    lane = lax.broadcasted_iota(jnp.int32, (size, blocks * group // 2), 1)
    place = (line // group == lane & (blocks - 1)) & ((line & (group - 1)) // 2 == lane // blocks)
    even = jnp.where(place & ((line & 1) == 0), 1.0, 0.0)
    odd = jnp.where(place & ((line & 1) == 1), 1.0, 0.0)
    return [m.astype(jnp.bfloat16) for m in (left, even, odd)]


def over_blocks(row, blocks):
    lane = lax.broadcasted_iota(jnp.int32, row.shape, 1)
    width = row.shape[1]
    shift = blocks // 2
    while shift > 0:
        up = pltpu.roll(row, shift, 1)
        down = pltpu.roll(row, width - shift, 1)
        row = row + jnp.where((lane & shift) == 0, down, up)
        shift //= 2
    return row


def kernel(
    n,
    n_space,
    snap_ref,
    closing_ref,
    weights_ref,
    bins_ref,
    out_ref,
    series,
    table_ref,
    left_ref,
    even_ref,
    odd_ref,
    a_high,
    a_low,
    b_high,
    b_low,
    gram,
    final,
    part,
    rows_in,
    weights,
    bins,
    local_sem,
    send_sem,
    recv_sem,
    part_send,
    part_recv,
    round_sem,
):
    me = lax.axis_index("tm")
    here = lax.axis_index("space")
    rows, points = snap_ref.shape
    tail_rows = closing_ref.shape[0]
    tiles = points // LANES
    steps = series.shape[0]
    pairs = steps - 1
    hop = NFFT // 2
    blocks_all = n * rows // hop
    channels = 2 * bins_ref.shape[0]
    group = channels // n
    own_rows = blocks_all // n_space

    deep = n // 2
    z, x = me // 2, lax.rem(me, 2)
    near = me // deep * deep
    far = deep - near

    def peer_of(k):
        return lax.rem(me + k, n)

    def begin(device):
        return tile_start(device, tiles, n, here)

    my_start = begin(me)
    my_last = begin(me + 1) - my_start == 2 * steps

    def rows_of(device):
        return pl.ds(pl.multiple_of(device * rows, rows), rows)

    def columns(start, count):
        return pl.ds(pl.multiple_of(start * LANES, LANES), count * LANES)

    def pair_copy(step, peer, sender):
        return pltpu.make_async_remote_copy(
            src_ref=snap_ref.at[:, columns(begin(peer) + 2 * step, 2)],
            dst_ref=series.at[step, rows_of(sender)],
            send_sem=send_sem.at[step, peer],
            recv_sem=recv_sem.at[step, sender],
            device_id={"tm": peer},
            device_id_type=MESH,
        )

    def half_copy(half, peer, sender, cut=0, cuts=1):
        size = rows // cuts
        first = pl.multiple_of(sender * rows + cut * size, size)
        source = columns(begin(peer) + 2 * pairs + half, 1)
        return pltpu.make_async_remote_copy(
            src_ref=snap_ref.at[pl.ds(cut * size, size), source],
            dst_ref=series.at[pairs, pl.ds(first, size), pl.ds(half * LANES, LANES)],
            send_sem=send_sem.at[pairs + half, peer],
            recv_sem=recv_sem.at[pairs + half, sender],
            device_id={"tm": peer},
            device_id_type=MESH,
        )

    def has_last(device):
        return begin(device + 1) - begin(device) == 2 * steps

    def own_pair(step):
        source = columns(my_start + 2 * step, 2)
        return (
            pltpu.make_async_copy(
                snap_ref.at[:, source], series.at[step, rows_of(me)], local_sem.at[0, step]
            ),
            pltpu.make_async_copy(
                closing_ref.at[:, source],
                series.at[step, pl.ds(n * rows, tail_rows)],
                local_sem.at[1, step],
            ),
        )

    def own_half(half):
        source = columns(my_start + 2 * pairs + half, 1)
        lanes = pl.ds(half * LANES, LANES)
        return (
            pltpu.make_async_copy(
                snap_ref.at[:, source],
                series.at[pairs, rows_of(me), lanes],
                local_sem.at[0, pairs + half],
            ),
            pltpu.make_async_copy(
                closing_ref.at[:, source],
                series.at[pairs, pl.ds(n * rows, tail_rows), lanes],
                local_sem.at[1, pairs + half],
            ),
        )

    weights_copy = pltpu.make_async_copy(weights_ref, weights, local_sem.at[2, 0])
    bins_copy = pltpu.make_async_copy(bins_ref, bins, local_sem.at[2, 1])

    def greet(sem):
        pl.semaphore_signal(sem, inc=1, device_id={"tm": me + 1 - 2 * x}, device_id_type=MESH)

        @pl.when(z + 1 < deep)
        def _():
            pl.semaphore_signal(sem, inc=1, device_id={"tm": me + 2}, device_id_type=MESH)

        @pl.when(z > 0)
        def _():
            pl.semaphore_signal(sem, inc=1, device_id={"tm": me - 2}, device_id_type=MESH)

        for other in (here + 1 - 2 * lax.rem(here, 2), lax.rem(here + 2, n_space)):
            pl.semaphore_signal(sem, inc=1, device_id={"space": other}, device_id_type=MESH)
        pl.semaphore_wait(sem, 3 + (z + 1 < deep).astype(jnp.int32) + (z > 0).astype(jnp.int32))

    def hops(peer):
        return jnp.abs(peer // 2 - z) + jnp.abs(lax.rem(peer, 2) - x)

    for reach in range(1, deep + 1):
        greet(pltpu.get_barrier_semaphore() if reach == 1 else round_sem.at[reach - 2])
        for k in range(1, n):
            peer = peer_of(k)

            @pl.when(hops(peer) == reach)
            def _(peer=peer):
                pair_copy(0, peer, me).start()

    @pl.loop(1, pairs)
    def _(step):
        for k in [3, 4, 5, 6, 7, 1, 2]:
            pair_copy(step, peer_of(k), me).start()

    for k in [3, 4, 5, 6, 7, 1, 2]:
        half_copy(0, peer_of(k), me).start()
    for cut in range(4):
        for k in [3, 4, 5, 6, 7, 1, 2]:

            @pl.when(has_last(peer_of(k)))
            def _(k=k, cut=cut):
                half_copy(1, peer_of(k), me, cut, 4).start()

    @pl.loop(0, pairs)
    def _(step):
        for copy in own_pair(step):
            copy.start()

    for copy in own_half(0):
        copy.start()

    @pl.when(my_last)
    def _():
        for copy in own_half(1):
            copy.start()

    weights_copy.start()
    bins_copy.start()
    for reach in range(deep + 1, deep + 3):
        greet(round_sem.at[reach - 2])

    gram[...] = jnp.zeros(gram.shape, jnp.float32)
    left_ref[...], even_ref[...], odd_ref[...] = selections(blocks_all, group, n_space)
    bins_copy.wait()
    channel = lax.broadcasted_iota(jnp.int32, (channels, 1), 0)
    held = jnp.zeros((channels, 1), jnp.int32)
    for k in range(channels // 2):
        held = jnp.where(channel // 2 == k, bins[k], held)
    table_high, table_low = halves(table_rows(held, NFFT))
    table_ref[:channels] = table_high
    table_ref[channels:] = table_low
    weights_copy.wait()

    def transform(step, lanes, weight, half=False):
        def run(turn, carry):
            block = lax.rem(near * (rows // hop) + turn, blocks_all)
            window = pl.ds(pl.multiple_of(block * hop, hop), NFFT)
            high, low = halves(series[step, window, lanes])
            both = matmul(table_ref[...], high)
            coef = both[:channels] + both[channels:] + matmul(table_ref[:channels], low)
            first_high, first_low = halves(coef)
            second_high, second_low = halves(coef * weight)
            place = pl.ds(pl.multiple_of(block * group, group), group)
            for g in range(n):
                cut = slice(g * group, (g + 1) * group)
                if half:
                    a_high[g, place, :LANES] = first_high[cut]
                    a_high[g, place, LANES:] = first_low[cut]
                    b_high[g, place, :LANES] = second_high[cut]
                    b_low[g, place, :LANES] = second_low[cut]
                else:
                    a_high[g, place, :] = first_high[cut]
                    a_low[g, place, :] = first_low[cut]
                    b_high[g, place, :] = second_high[cut]
                    b_low[g, place, :] = second_low[cut]
            return carry

        return run

    def products(g, carry):
        gram[g] += (
            matmul_nt(b_high[g], a_high[g])
            + matmul_nt(b_high[g], a_low[g])
            + matmul_nt(b_low[g], a_high[g])
        )
        return carry

    def half_product(g):
        first, second = a_high[g], b_high[g, :, :LANES]
        return matmul_nt(jnp.concatenate([second, second], axis=1), first) + matmul_nt(
            b_low[g, :, :LANES], first[:, :LANES]
        )

    ready = blocks_all // 2 - 1

    def near_peer(k):
        return near + lax.rem(me - near + k, deep)

    @pl.loop(0, pairs)
    def _(step):
        weight = weights[pl.ds(pl.multiple_of((my_start + 2 * step) * LANES, LANES), 2 * LANES)]
        run = transform(step, slice(0, 2 * LANES), weight.reshape(1, 2 * LANES))
        for copy in own_pair(step):
            copy.wait()
        for k in range(1, deep):
            pair_copy(step, me, near_peer(k)).wait_recv()
        lax.fori_loop(0, ready, run, 0, unroll=ready)
        for k in range(deep):
            pair_copy(step, me, far + k).wait_recv()
        lax.fori_loop(ready, blocks_all, run, 0, unroll=3)
        lax.fori_loop(0, n, products, 0, unroll=2)

    def last(half):
        lanes = slice(half * LANES, (half + 1) * LANES)
        tile = my_start + 2 * pairs + half
        weight = weights[pl.ds(pl.multiple_of(tile * LANES, LANES), LANES)]
        run = transform(pairs, lanes, weight.reshape(1, LANES), half=True)
        for copy in own_half(half):
            copy.wait()
        for k in range(1, deep):
            half_copy(half, me, near_peer(k)).wait_recv()
        lax.fori_loop(0, ready, run, 0, unroll=ready)
        for k in range(deep):
            half_copy(half, me, far + k).wait_recv()
            stop = blocks_all if k == deep - 1 else ready + 2 + 2 * k
            first = ready + 2 * k
            lax.fori_loop(first, stop, run, 0, unroll=stop - first)

    last(0)

    def half_products(g, carry):
        gram[g] += half_product(g)
        return carry

    lax.fori_loop(0, n, half_products, 0, unroll=2)

    size = gram.shape[1]
    row = lax.broadcasted_iota(jnp.int32, (size, size), 0)
    col = lax.broadcasted_iota(jnp.int32, (size, size), 1)
    same_bin = ((row & (group - 1)) >> 1) == ((col & (group - 1)) >> 1)
    line = lax.broadcasted_iota(jnp.int32, part.shape[1:], 0)
    lane = lax.broadcasted_iota(jnp.int32, part.shape[1:], 1)
    imag_row = ((line // own_rows) & 1) == 1
    held_row = line // (2 * own_rows) * own_rows + (line & (own_rows - 1))
    on_diagonal = held_row == lane & (blocks_all - 1)

    def fold(k):
        kept = picked(left_ref[...], jnp.where(same_bin, final[k], 0.0))
        middle = kept.shape[0] // 2
        sums = picked_right(kept[:middle], even_ref[...]) + picked_right(
            kept[middle:], odd_ref[...]
        )
        real = jnp.where(on_diagonal & ~imag_row, sums, 0.0)
        trace = over_blocks(jnp.sum(real, axis=0, keepdims=True), blocks_all)
        part[k] = jnp.where(on_diagonal & imag_row, trace, sums)

    @pl.when(my_last)
    def _():
        last(1)

    def finish(k, g):
        final[k] = gram[g] + jnp.where(my_last, half_product(g), 0.0)

    own_lines = 2 * own_rows

    def part_copy(k, peer, there, sender, sender_space):
        return pltpu.make_async_remote_copy(
            src_ref=part.at[k, pl.ds(there * own_lines, own_lines)],
            dst_ref=rows_in.at[sender, sender_space],
            send_sem=part_send.at[k, there],
            recv_sem=part_recv.at[sender, sender_space],
            device_id={"tm": peer, "space": there},
            device_id_type=MESH,
        )

    def part_arrival(sender, sender_space):
        return part_copy(0, sender, 0, sender, sender_space)

    for k in range(deep):
        finish(k, far + k)
    for k in range(deep):
        fold(k)
    for k in range(deep):
        finish(deep + k, near + k)
    for k in range(deep):
        for there in range(n_space):
            part_copy(k, far + k, there, me, here).start()
    for k in range(deep, n):
        fold(k)
    for k in range(deep):
        for there in range(n_space):

            @pl.when((near + k != me) | (here != there))
            def _(k=k, there=there):
                part_copy(deep + k, near + k, there, me, here).start()

    @pl.loop(0, pairs)
    def _(step):
        for k in range(1, n):
            pair_copy(step, peer_of(k), me).wait_send()

    for k in range(1, n):
        half_copy(0, peer_of(k), me).wait_send()

        @pl.when(has_last(peer_of(k)))
        def _(k=k):
            half_copy(1, peer_of(k), me).wait_send()

    own = pl.ds(pl.multiple_of(here * own_lines, own_lines), own_lines)
    rows_in[me, here] = part[deep + me - near, own]
    for k in range(deep):
        for there in range(n_space):
            part_copy(k, far + k, there, me, here).wait_send()

            @pl.when((near + k != me) | (here != there))
            def _(k=k, there=there):
                part_copy(deep + k, near + k, there, me, here).wait_send()

    for k in range(deep):
        for there in range(n_space):

            @pl.when((near + k != me) | (here != there))
            def _(k=k, there=there):
                part_arrival(near + k, there).wait_recv()

    for k in range(deep):
        for there in range(n_space):
            part_arrival(far + k, there).wait_recv()
    total = rows_in[0, 0]
    for p in range(n):
        for q in range(n_space):
            if p + q > 0:
                total = total + rows_in[p, q]
    line = lax.broadcasted_iota(jnp.int32, total.shape, 0)
    block = lax.broadcasted_iota(jnp.int32, total.shape, 1) & (blocks_all - 1)
    first = (line == own_rows) & (block == here * own_rows)
    held = jnp.sum(jnp.where(first, total, 0.0), axis=0, keepdims=True)
    energy = over_blocks(held, blocks_all)
    zero = (line >= own_rows) & (block == here * own_rows + (line & (own_rows - 1)))
    spectra = jnp.where(zero, 0.0, total) * (blocks_all / energy)
    for b in range(group // 2):
        out_ref[b] = spectra[:, b * blocks_all : (b + 1) * blocks_all].reshape(out_ref.shape[1:])


def fused_body(snapshots, closing, weights, bin_index):
    n, n_space = lax.axis_size("tm"), lax.axis_size("space")
    rows, points = snapshots.shape
    tail_rows = closing.shape[0]
    tiles = points // LANES
    steps = -(-tiles // n) // 2
    blocks_all = n * rows // (NFFT // 2)
    channels = 2 * bin_index.shape[0]
    group = channels // n
    size = blocks_all * group
    own_rows = blocks_all // n_space
    shape = (2 * own_rows, size // 2)
    return pl.pallas_call(
        functools.partial(kernel, n, n_space),
        out_shape=pltpu.VMEM((group // 2, 2, own_rows, blocks_all), jnp.float32),
        in_specs=[pl.BlockSpec(memory_space=pl.ANY)] * 4,
        out_specs=pl.BlockSpec(memory_space=pltpu.VMEM),
        scratch_shapes=[
            pltpu.VMEM((steps, n * rows + tail_rows, 2 * LANES), jnp.float32),
            pltpu.VMEM((2 * channels, NFFT), jnp.bfloat16),
            pltpu.VMEM((4 * blocks_all, size), jnp.bfloat16),
            pltpu.VMEM((size, size // 2), jnp.bfloat16),
            pltpu.VMEM((size, size // 2), jnp.bfloat16),
        ]
        + [pltpu.VMEM((n, size, 2 * LANES), jnp.bfloat16)] * 4
        + [
            pltpu.VMEM((n, size, size), jnp.float32),
            pltpu.VMEM((n, size, size), jnp.float32),
            pltpu.VMEM((n, 2 * blocks_all, size // 2), jnp.float32),
            pltpu.VMEM((n, n_space) + shape, jnp.float32),
            pltpu.VMEM((points,), jnp.float32),
            pltpu.SMEM((channels // 2,), jnp.int32),
            pltpu.SemaphoreType.DMA((3, steps + 1)),
            pltpu.SemaphoreType.DMA((steps + 1, n)),
            pltpu.SemaphoreType.DMA((steps + 1, n)),
            pltpu.SemaphoreType.DMA((n, n_space)),
            pltpu.SemaphoreType.DMA((n, n_space)),
            pltpu.SemaphoreType.REGULAR((n // 2 + 1,)),
        ],
        compiler_params=pltpu.CompilerParams(collective_id=0, has_side_effects=True),
    )(snapshots, closing, weights, bin_index)


def chosen_body(snapshots, closing, weights, bin_index):
    n, n_space = lax.axis_size("tm"), lax.axis_size("space")
    rows, points = snapshots.shape
    group = 2 * NBINS // n
    blocks_all = n * rows // (NFFT // 2)
    tiles = points // LANES
    slots = -(-tiles // n)
    fits = (
        2 * NBINS % n == 0
        and n % 2 == 0
        and n_space == 4
        and points % LANES == 0
        and slots % 2 == 0
        and slots > 2
        and tiles // n >= slots - 1
        and closing.shape[0] == NFFT // 2
        and rows == NFFT
        and group == 16
        and blocks_all == 16
    )
    return (fused_body if fits else body)(snapshots, closing, weights, bin_index)


def solution(mesh):
    return jax.shard_map(
        chosen_body,
        mesh=mesh,
        in_specs=(P("tm", "space"), P(None, "space"), P("space"), P()),
        out_specs=P("tm", None, "space", None),
        check_vma=False,
    )
```
